32 devices in a mesh: space: 16 (over z, y, x), mem: 2 (over core).
Axes of the slice: x: 2, y: 2, z: 4, core: 2. Of those that a mesh axis runs over, the one named last changes fastest.
Arguments:
- perturb: float32 [1024, 4096], P(('space', 'mem')), may hold values from -6 to 6
- pair_list: int32 [64, 3], P('space'), may hold values from 0 to 15, as said below
- pair_count: int32 [16], P('space'), may hold values from 1 to 4, as said below
- band_weight: float32 [8], replicated, may hold values from 0.25 to 1
- cov_scale: float32 [1], replicated, may hold values from 0.5 to 2
- target: float32 [4096, 1024], P('space', 'mem'), may hold values from -6 to 6
- first_guess: float32 [4096, 1024], P('space', 'mem'), may hold values from -6 to 6
Outputs:
- solution: float32 [4096, 1024], P('space', 'mem')
The draws below stay inside these ranges and needn't reach their ends.
Inputs may be any that keep to these rules, and one draw needn't show every extreme that they name: `pair_list`: rows 4 * s to 4 * s + 3 are owner s's slots. The first block of each is owner s's own block s; the second is the first plus d modulo 16, with 0 <= d <= 3; each of the four pairs (d = 0 to 3) stands in exactly one slot of its owner. The third column is an index into band_weight. Only the first pair_count[s] slots of owner s are live; in every draw some owner has all 4 slots live.
All inputs are finite; a program needn't handle non-finite values.
Results may differ from the reference program's by a relative error of at most 0.0003.
Values sent between devices are 32-bit elements; how exact they have to be, the bound alone decides.
A program may use at most 64 MiB of HBM per device.

```python
import math
import jax
import jax.numpy as jnp
from jax import lax

BLOCK = 256
MEMBERS = 1024
COLS = 1024
BLK_DEV = 1
REACH_DEV = 3
NBANDS = 8
ITERS = 2
CAP = 4
ROWS = 4096
NBLK = 16
PAIRS = 64


def pair_tables(key):
    owners = PAIRS // CAP
    reach = REACH_DEV * BLK_DEV
    subkeys = jax.random.split(jax.random.fold_in(key, 11), owners)
    orders = jax.vmap(lambda subkey: jax.random.permutation(subkey, CAP))(subkeys).astype(jnp.int32)
    starts = (jnp.arange(owners, dtype=jnp.int32) * BLK_DEV)[:, None]
    first_block = starts + orders // (reach + 1)
    gap = orders % (reach + 1)
    second_block = (first_block + gap) % NBLK
    jitter = jax.random.randint(jax.random.fold_in(key, 12), (owners, CAP), 0, 2)
    band = jnp.minimum(NBANDS - 1, gap * 4 // reach + jitter)
    pairs = jnp.stack([first_block, second_block, band], -1).reshape(PAIRS, 3).astype(jnp.int32)
    lower = jax.random.randint(jax.random.fold_in(key, 13), (owners,), 1, CAP + 1)
    upper = jax.random.randint(jax.random.fold_in(key, 14), (owners,), 1, CAP + 1)
    counts = jnp.minimum(lower, upper)
    hottest = jax.random.randint(jax.random.fold_in(key, 15), (), 0, owners)
    counts = counts.at[hottest].set(CAP).astype(jnp.int32)
    return (pairs, counts)


def draw_pair_list(key, part):
    return pair_tables(jax.random.fold_in(key, 7))[0]


def draw_pair_count(key, part):
    return pair_tables(jax.random.fold_in(key, 7))[1]


def level_of(rng, shape, cuts, least, top_value):
    def one(position, blocks):
        heights = jax.random.uniform(jax.random.fold_in(jax.random.fold_in(rng, 6), position), (blocks,), jnp.float32, least / len(cuts), top_value / len(cuts))
        return jnp.repeat(jnp.exp(heights), shape[position] // blocks).reshape((-1,) + (1,) * (len(shape) - position - 1))

    factor_of = one(*cuts[0])
    for cut in cuts[1:]:
        factor_of = factor_of * one(*cut)
    return factor_of


def bell_draw(own_key, extent, spread, limit, cuts=(), kind=jnp.bfloat16):
    array = spread * jax.random.normal(own_key, extent, jnp.float32)
    if cuts:
        array = array * level_of(own_key, extent, cuts, -0.22, 0.18)
    return jnp.clip(array, -limit, limit).astype(kind)


def setup_inputs(seed: int = 0) -> dict:
    splits = jax.random.split(jax.random.key(seed), 8)
    perturb = bell_draw(splits[0], (MEMBERS, ROWS), 1.0, 6.0, ((0, 32),), jnp.float32)
    pair_list = draw_pair_list(jax.random.fold_in(splits[7], 71), 0)
    pair_count = draw_pair_count(jax.random.fold_in(splits[7], 71), 0)
    band_weight = jnp.clip(jnp.exp(jax.random.uniform(splits[3], (NBANDS,), jnp.float32, math.log(0.25), math.log(1.0))), 0.25, 1.0)
    cov_scale = jnp.clip(jax.random.uniform(splits[4], (1,), jnp.float32, 0.5, 2.0), 0.5, 2.0)
    target = bell_draw(splits[5], (ROWS, COLS), 1.0, 6.0, ((0, 16), (1, 2)), jnp.float32)
    first_guess = bell_draw(splits[6], (ROWS, COLS), 1.0, 6.0, ((0, 16), (1, 2)), jnp.float32)
    return dict(perturb=perturb, pair_list=pair_list, pair_count=pair_count, band_weight=band_weight, cov_scale=cov_scale, target=target, first_guess=first_guess)


def reference(perturb, pair_list, pair_count, band_weight, cov_scale, target, first_guess):
    numbers = jnp.arange(PAIRS, dtype=jnp.int32)
    owners = numbers // CAP
    slot_ids = numbers % CAP
    living = (slot_ids < pair_count[owners]).astype(jnp.float32)
    weights = cov_scale[0] * band_weight[pair_list[:, 2]] * living / (MEMBERS - 1)

    def build_tile(number):
        first_cols = lax.dynamic_slice_in_dim(perturb, (pair_list[number, 0] * BLOCK).astype(jnp.int32), BLOCK, 1)
        second_cols = lax.dynamic_slice_in_dim(perturb, (pair_list[number, 1] * BLOCK).astype(jnp.int32), BLOCK, 1)
        return jnp.dot(first_cols.T, second_cols, precision=lax.Precision.HIGHEST, preferred_element_type=jnp.float32) * weights[number]

    tiles = lax.map(build_tile, numbers)

    def apply_cov(iterate):
        def advance(running, number):
            first_row = (pair_list[number, 0] * BLOCK).astype(jnp.int32)
            second_row = (pair_list[number, 1] * BLOCK).astype(jnp.int32)
            tile_now = tiles[number]
            own_rows = lax.dynamic_slice_in_dim(iterate, first_row, BLOCK, 0)
            near_rows = lax.dynamic_slice_in_dim(iterate, second_row, BLOCK, 0)
            forward = jnp.dot(tile_now, near_rows, precision=lax.Precision.HIGHEST, preferred_element_type=jnp.float32)
            mirror = jnp.dot(tile_now.T, own_rows, precision=lax.Precision.HIGHEST, preferred_element_type=jnp.float32)
            mirror = mirror * (pair_list[number, 0] != pair_list[number, 1]).astype(jnp.float32)
            running = lax.dynamic_update_slice_in_dim(running, lax.dynamic_slice_in_dim(running, first_row, BLOCK, 0) + forward, first_row, 0)
            running = lax.dynamic_update_slice_in_dim(running, lax.dynamic_slice_in_dim(running, second_row, BLOCK, 0) + mirror, second_row, 0)
            return running, None

        total, unused = lax.scan(advance, jnp.zeros_like(iterate), numbers)
        return total

    iterate = first_guess
    for sweep in range(ITERS):
        iterate = iterate + 0.5 * (target - iterate - apply_cov(iterate))
    return iterate
```

```python
import functools
import jax
import jax.numpy as jnp
from jax import lax
from jax.experimental import pallas as pl
from jax.experimental.pallas import tpu as pltpu
from jax.sharding import PartitionSpec as P

BLOCK = 256
MEMBERS = 1024
REACH_DEV = 3
NBANDS = 8
ITERS = 2


def shifted(array, axis, by):
    count = lax.axis_size(axis)
    return lax.ppermute(array, axis, [(i, (i + by) % count) for i in range(count)])


def mm(a, b, ca, cb):
    return lax.dot_general(
        a, b, (((ca,), (cb,)), ((), ())), precision=lax.Precision.HIGH,
        preferred_element_type=jnp.float32,
    )


def member_sum(tile):
    if lax.axis_size("mem") == 2:
        return tile + shifted(tile, "mem", 1)
    return lax.psum(tile, "mem")


def gap_weights(pair_list, pair_count, band_weight, cov_scale):
    slots = pair_list.shape[0]
    blocks_all = lax.axis_size("space")
    gap = (pair_list[:, 1] - pair_list[:, 0]) % blocks_all
    living = (jnp.arange(slots, dtype=jnp.int32) < pair_count[0]).astype(jnp.float32)
    bands = jnp.arange(NBANDS, dtype=jnp.int32)
    band_now = jnp.sum(
        jnp.where(pair_list[:, 2][:, None] == bands[None, :], band_weight[None, :], 0.0), axis=1
    )
    slot_weight = cov_scale[0] * band_now * living / (MEMBERS - 1)
    gaps = jnp.arange(REACH_DEV + 1, dtype=jnp.int32)
    return jnp.sum(jnp.where(gap[:, None] == gaps[None, :], slot_weight[:, None], 0.0), axis=0)


def by_collectives(perturb, pair_list, pair_count, band_weight, cov_scale, target, first_guess):
    w = gap_weights(pair_list, pair_count, band_weight, cov_scale)
    w_next = shifted(w, "space", -1)
    p0 = lax.all_to_all(perturb, "space", split_axis=1, concat_axis=0, tiled=True)
    p1 = shifted(p0, "space", -1)
    p3 = shifted(p0, "space", -3)
    x0 = first_guess
    t0 = mm(p0, p0, 0, 0) * w[0]
    t1 = mm(p0, p1, 0, 0) * w[1]
    t3 = mm(p0, p3, 0, 0) * w[3]
    t2 = mm(p1, p3, 0, 0) * w_next[2]
    t0, t1, t2, t3 = (member_sum(t) for t in (t0, t1, t2, t3))
    for sweep in range(ITERS):
        x1 = shifted(x0, "space", -1)
        x3 = shifted(x0, "space", -3)
        back1 = shifted(mm(t1, x0, 0, 0) + mm(t2, x3, 1, 0), "space", 1)
        back3 = shifted(mm(t3, x0, 0, 0) + mm(t2, x1, 0, 0), "space", 3)
        own = mm(t0, x0, 1, 0) + mm(t1, x1, 1, 0) + mm(t3, x3, 1, 0)
        x0 = x0 + 0.5 * (target - x0 - (own + back1 + back3))
    return x0

GROUP = REACH_DEV + 1
NEAR = 2 * REACH_DEV + 1
PLANES = 4


def split(value):
    high = value.astype(jnp.bfloat16)
    return high, (value - high.astype(jnp.float32)).astype(jnp.bfloat16)


def dot(a, b, ca, cb):
    return lax.dot_general(a, b, (((ca,), (cb,)), ((), ())), preferred_element_type=jnp.float32)


class Mover:
    def __init__(self, send_sem, recv_sem, local_sem):
        self.send_sem, self.recv_sem, self.local_sem = send_sem, recv_sem, local_sem
        self.used = 0
        self.local = 0
        self.open = []

    def reserve(self, number):
        first = self.used
        self.used += number
        return first

    def make(self, source, target, device, send, recv):
        return pltpu.make_async_remote_copy(
            src_ref=source, dst_ref=target,
            send_sem=self.send_sem.at[send], recv_sem=self.recv_sem.at[recv],
            device_id=device, device_id_type=pl.DeviceIdType.MESH,
        )

    def to(self, source, target, device, send=None, recv=None):
        if send is None:
            send = recv = self.reserve(1)
        copy = self.make(source, target, device, send, recv)
        copy.start()
        self.open.append(copy)
        return copy

    def here(self, source, target):
        copy = pltpu.make_async_copy(source, target, self.local_sem.at[self.local])
        self.local += 1
        copy.start()
        return copy


def kernel(perturb, table, guess, target, out, gc, gb, chi, clo, bhi, blo, part, tile_hi, tile_lo,
           tabs, xb, tb, halo, xs, acc, px, ret_in, ahead, final, send_sem, recv_sem, local_sem):
    space = lax.axis_index("space")
    mem = lax.axis_index("mem")
    k = space // GROUP
    j = space % GROUP
    rows = perturb.shape[0]
    half = rows // 2
    cols = xb.shape[2]
    B = BLOCK
    wide = REACH_DEV * B
    inner = GROUP * B
    each = 2 * GROUP * rows

    def plane(p):
        return (p * GROUP + j, mem)

    def chip(q):
        return (k * GROUP + q, mem)

    xn = chip(j + 1 - 2 * (j % 2))
    yn = chip((j + 2) % GROUP)
    partner = (space, 1 - mem)
    before = plane((k + PLANES - 1) % PLANES)
    after = plane((k + 1) % PLANES)

    barrier = pltpu.get_barrier_semaphore()
    greeted = [plane((k + r) % PLANES) for r in range(1, PLANES)]
    greeted += [chip((j + q) % GROUP) for q in range(1, GROUP)] + [partner]
    for device in greeted:
        pl.semaphore_signal(barrier, inc=1, device_id=device, device_id_type=pl.DeviceIdType.MESH)

    move = Mover(send_sem, recv_sem, local_sem)

    def at(block, size):
        return pl.ds(pl.multiple_of(block * B, B), size * B)

    def piece(q):
        return pl.ds(pl.multiple_of(q * cols, cols), cols)

    def pieces(p, slot):
        first = p * GROUP
        after_first = ((p + 1) % PLANES) * GROUP
        return (
            (perturb.at[:, at(first + 1, REACH_DEV)], gc.at[slot, 0, 0, :, pl.ds(0, wide)]),
            (perturb.at[:, at(after_first, REACH_DEV)], gc.at[slot, 0, 0, :, pl.ds(wide, wide)]),
            (perturb.at[:, at(first, 1)], gb.at[0, 0, slot]),
        )

    own_here = [move.here(*pair) for pair in pieces(k, 0)]
    x_here = move.here(guess.at[:, piece(j)], xb.at[j])
    t_here = move.here(target.at[:, piece(j)], tb.at[j])
    tab_here = move.here(table, tabs.at[j])
    pl.semaphore_wait(barrier, len(greeted))

    zsem = move.reserve(3 * PLANES)
    other_half = 2 - 2 * (k // 2)
    late = 2 + (k + k // 2 + 1) % 2
    routes = ((k + 1 - 2 * (k % 2), 1), (other_half, late), (other_half + 1, late))

    def exchange(which):
        for n, (p, slot) in enumerate(routes):
            for m in which:
                source, place = pieces(p, slot)[m]
                move.to(source, place, plane(p), zsem + 3 * n + m, zsem + 3 * slot + m)

    def from_plane(slot, which):
        for m in which:
            place = pieces(k, slot)[m][1]
            move.make(place, place, before, zsem, zsem + 3 * slot + m).wait_recv()

    exchange((0, 1))
    for copy in own_here:
        copy.wait()

    class Gather:
        def __init__(self, buffer, cut):
            self.buffer, self.cut = buffer, cut

        def own(self):
            source = self.buffer.at[0, 0]
            self.cx = move.to(source, self.buffer.at[1, 0], xn)
            self.cy = move.to(source, self.buffer.at[2, 0], yn)
            self.done = [move.to(source, self.buffer.at[0, 1], partner)]

        def over(self, q):
            self.done.append(move.to(self.buffer.at[q, 0], self.buffer.at[q, 1], partner))

        def relay(self):
            low, high = pl.ds(0, self.cut), pl.ds(self.cut, self.cut)
            self.cx.wait_recv()
            first = move.to(self.buffer.at[1, 0, low], self.buffer.at[3, 0, low], yn)
            self.over(1)
            self.cy.wait_recv()
            second = move.to(self.buffer.at[2, 0, high], self.buffer.at[3, 0, high], xn)
            self.over(2)
            self.halves = (first, second)

        def corner(self):
            for copy in self.halves:
                copy.wait_recv()
            self.over(3)

        def ready(self):
            for copy in self.done:
                copy.wait_recv()

    cross = [Gather(gc.at[r], half) for r in range(PLANES)]
    edge = Gather(gb, PLANES // 2)
    cross[0].own()
    tab_here.wait()
    tab_copies = [move.to(tabs.at[j], tabs.at[j], chip((j + q) % GROUP)) for q in range(1, GROUP)]

    def share(source, blocks):
        copies = []
        for q in range(1, GROUP):
            there = (j + q) % GROUP
            copies.append(move.to(source.at[:, piece(there)], blocks.at[j], chip(there)))
        return copies

    x_copies = share(guess, xb)
    exchange((2,))

    def weight(a, d):
        return tabs[a, d : d + 1]

    def products(r):
        span = pl.ds(r * each, each)
        chi[span], clo[span] = split(gc[r].reshape(each, 2 * wide))

        def step(n, carry):
            own = pl.ds(pl.multiple_of(n * B, B), B)
            row = pl.ds(pl.multiple_of(n * B, B), inner)
            left = jnp.concatenate([chi[span, own], chi[span, own], clo[span, own]], 0)
            right = jnp.concatenate([chi[span, row], clo[span, row], chi[span, row]], 0)
            value = dot(left, right, 0, 0)
            if r > 0:
                value = value + part[n]
            if r < PLANES - 1:
                part[n] = value
            else:
                for d in range(GROUP):
                    now = value[:, d * B : (d + 1) * B] * weight(n + 1, d)
                    there = pl.ds(d * B, B)
                    tile_hi[n + 1, :, there], tile_lo[n + 1, :, there] = split(now)
            return carry

        lax.fori_loop(0, REACH_DEV, step, 0)

    def edge_products():
        for r in range(PLANES):
            span = pl.ds(r * each, each)
            bhi[span], blo[span] = split(gb[:, :, r].reshape(each, B))
        left = jnp.concatenate([bhi[...], bhi[...], blo[...]], 0)
        right = jnp.concatenate([bhi[...], blo[...], bhi[...]], 0)
        now = dot(left, right, 0, 0) * weight(0, 0)
        tile_hi[0, :, :B], tile_lo[0, :, :B] = split(now)
        for d in range(1, GROUP):
            there = pl.ds((d - 1) * B, B)
            right = jnp.concatenate([chi[:, there], clo[:, there], chi[:, there]], 0)
            now = dot(left, right, 0, 0) * weight(0, d)
            place = pl.ds(d * B, B)
            tile_hi[0, :, place], tile_lo[0, :, place] = split(now)

    def times(high, low, x, side):
        both = dot(high, x, side, 0)
        return both[:, :cols] + both[:, cols:] + dot(low, x[:, :cols], side, 0)

    def block(n, size=1):
        return pl.ds(n * B, size * B)

    def set_x(n, value):
        xs[block(n), :cols], xs[block(n), cols:] = split(value)

    def forward(a, d, size):
        span = pl.ds(d * B, size * B)
        return times(tile_hi[a, :, span], tile_lo[a, :, span], xs[block(a + d, size)], 1)

    def down(a):
        span = pl.ds(B, wide)
        return times(tile_hi[a, :, span], tile_lo[a, :, span], xs[block(a)], 0)

    def outgoing(sweep):
        acc[sweep, block(4, 3)] = down(3)
        low = down(2)
        acc[sweep, block(3)] = low[:B]
        acc[sweep, block(4, 2)] += low[B:]
        low = down(1)
        acc[sweep, block(2)] = low[:B]
        acc[sweep, block(3, 2)] += low[B:]
        return [
            move.to(acc.at[sweep, block(GROUP + n)], ret_in.at[sweep, n], after)
            for n in range(REACH_DEV)
        ]

    for slot in range(1, PLANES):
        from_plane(slot, (0, 1))
        cross[slot].own()
        cross[slot - 1].relay()
        if slot >= 2:
            cross[slot - 2].corner()
        if slot == 2:
            for copy in x_copies:
                copy.wait_recv()
            x_here.wait()
            halo_copy = move.to(xb.at[pl.ds(0, REACH_DEV)], halo, before)
    for slot in range(1, PLANES):
        from_plane(slot, (2,))
    edge.own()
    cross[0].ready()
    products(0)
    cross[3].relay()
    t_copies = share(target, tb)
    cross[2].corner()
    edge.relay()
    cross[1].ready()
    products(1)
    for n in range(GROUP):
        set_x(n, xb[n])
    cross[3].corner()
    edge.corner()
    halo_copy.wait_recv()
    for n in range(REACH_DEV):
        set_x(GROUP + n, halo[n])
    cross[2].ready()
    products(2)
    for copy in tab_copies:
        copy.wait_recv()
    cross[3].ready()
    products(3)

    rets = outgoing(0)
    acc[0, block(3)] += forward(3, 0, GROUP)
    acc[0, block(2)] += forward(2, 0, GROUP)
    acc[0, block(1)] = forward(1, 0, GROUP)
    edge.ready()
    edge_products()
    acc[0, block(1, 3)] += down(0)
    acc[0, block(0)] = forward(0, 0, GROUP)
    for copy in t_copies:
        copy.wait_recv()
    t_here.wait()

    aheads = []

    def advance(n):
        change = acc[0, block(n)]
        if n < REACH_DEV:
            rets[n].wait_recv()
            change = change + ret_in[0, n]
        px[n] = xb[n] + 0.5 * (tb[n] - xb[n] - change)
        if n < REACH_DEV:
            aheads.append(move.to(px.at[n], ahead.at[n], before))
        set_x(n, px[n])

    advance(3)
    for n in range(REACH_DEV):
        advance(n)
    rets = outgoing(1)
    acc[1, block(1)] = forward(1, 0, 3)
    acc[1, block(2)] += forward(2, 0, 2)
    acc[1, block(3)] += forward(3, 0, 1)
    acc[1, block(1, 3)] += down(0)
    acc[1, block(0)] = forward(0, 0, GROUP)

    base = move.reserve(GROUP)
    here_sem = local_sem.at[move.local]

    def leave(n, source):
        return move.make(final.at[n], out.at[:, piece(j)], chip(n), base + n, base + source)

    def stay(n):
        return pltpu.make_async_copy(final.at[n], out.at[:, piece(j)], here_sem)

    def put(n):
        change = acc[1, block(n)]
        if n < REACH_DEV:
            rets[n].wait_recv()
            change = change + ret_in[1, n]
        final[n] = px[n] + 0.5 * (tb[n] - px[n] - change)

        @pl.when(j != n)
        def _():
            leave(n, j).start()

        @pl.when(j == n)
        def _():
            stay(n).start()

    for n in range(REACH_DEV):
        aheads[n].wait_recv()
        set_x(GROUP + n, ahead[n])
        for a in range(n + 1, GROUP):
            acc[1, block(a)] += forward(a, GROUP + n - a, 1)
    for n in (3, 0, 1, 2):
        put(n)
    for n in range(GROUP):
        @pl.when(j != n)
        def _():
            leave(n, n).wait_send()
            leave(n, n).wait_recv()

        @pl.when(j == n)
        def _():
            stay(n).wait()
    for copy in move.open:
        copy.wait_send()


def in_one_kernel(perturb, pair_list, pair_count, band_weight, cov_scale, target, first_guess):
    w = gap_weights(pair_list, pair_count, band_weight, cov_scale)
    table = jnp.broadcast_to(jnp.pad(w, (0, 8 - w.shape[0]))[:, None], (8, BLOCK))
    rows = perturb.shape[0]
    cols = first_guess.shape[1] // GROUP
    members = 2 * GROUP * PLANES * rows
    f32, bf16 = jnp.float32, jnp.bfloat16
    sems = 112
    vmem = pl.BlockSpec(memory_space=pltpu.VMEM)
    anywhere = pl.BlockSpec(memory_space=pl.ANY)
    return pl.pallas_call(
        kernel,
        out_shape=jax.ShapeDtypeStruct(first_guess.shape, f32),
        in_specs=[anywhere, vmem, anywhere, anywhere],
        out_specs=vmem,
        scratch_shapes=[
            pltpu.VMEM((PLANES, GROUP, 2, rows, 2 * REACH_DEV * BLOCK), f32),
            pltpu.VMEM((GROUP, 2, PLANES, rows, BLOCK), f32),
            pltpu.VMEM((members, 2 * REACH_DEV * BLOCK), bf16),
            pltpu.VMEM((members, 2 * REACH_DEV * BLOCK), bf16),
            pltpu.VMEM((members, BLOCK), bf16),
            pltpu.VMEM((members, BLOCK), bf16),
            pltpu.VMEM((REACH_DEV, BLOCK, GROUP * BLOCK), f32),
            pltpu.VMEM((GROUP, BLOCK, GROUP * BLOCK), bf16),
            pltpu.VMEM((GROUP, BLOCK, GROUP * BLOCK), bf16),
            pltpu.VMEM((GROUP, 8, BLOCK), f32),
            pltpu.VMEM((GROUP, BLOCK, cols), f32),
            pltpu.VMEM((GROUP, BLOCK, cols), f32),
            pltpu.VMEM((REACH_DEV, BLOCK, cols), f32),
            pltpu.VMEM((NEAR * BLOCK, 2 * cols), bf16),
            pltpu.VMEM((2, NEAR * BLOCK, cols), f32),
            pltpu.VMEM((GROUP, BLOCK, cols), f32),
            pltpu.VMEM((2, REACH_DEV, BLOCK, cols), f32),
            pltpu.VMEM((REACH_DEV, BLOCK, cols), f32),
            pltpu.VMEM((GROUP, BLOCK, cols), f32),
            pltpu.SemaphoreType.DMA((sems,)),
            pltpu.SemaphoreType.DMA((sems,)),
            pltpu.SemaphoreType.DMA((8,)),
        ],
        compiler_params=pltpu.CompilerParams(
            collective_id=0, has_side_effects=True, vmem_limit_bytes=56 * 1024 * 1024
        ),
    )(perturb, table, first_guess, target)


def fits(perturb, field):
    return (
        lax.axis_size("mem") == 2 and lax.axis_size("space") == PLANES * GROUP
        and perturb.shape[0] % 16 == 0 and field.shape[1] % (GROUP * 128) == 0
        and field.shape[0] == BLOCK
    )


def per_device(perturb, pair_list, pair_count, band_weight, cov_scale, target, first_guess):
    whole = in_one_kernel if fits(perturb, first_guess) else by_collectives
    return whole(perturb, pair_list, pair_count, band_weight, cov_scale, target, first_guess)


def solution(mesh):
    in_specs = (
        P(("space", "mem"), None),
        P("space", None),
        P("space"),
        P(),
        P(),
        P("space", "mem"),
        P("space", "mem"),
    )
    out_specs = P("space", "mem")
    return jax.shard_map(
        per_device, mesh=mesh, in_specs=in_specs, out_specs=out_specs, check_vma=False
    )
```

```python
import functools
import jax
import jax.numpy as jnp
from jax import lax
from jax.experimental import pallas as pl
from jax.experimental.pallas import tpu as pltpu
from jax.sharding import PartitionSpec as P

BLOCK = 256
MEMBERS = 1024
REACH_DEV = 3
NBANDS = 8
ITERS = 2


def shifted(array, axis, by):
    count = lax.axis_size(axis)
    return lax.ppermute(array, axis, [(i, (i + by) % count) for i in range(count)])


def mm(a, b, ca, cb):
    return lax.dot_general(
        a, b, (((ca,), (cb,)), ((), ())), precision=lax.Precision.HIGH,
        preferred_element_type=jnp.float32,
    )


def member_sum(tile):
    if lax.axis_size("mem") == 2:
        return tile + shifted(tile, "mem", 1)
    return lax.psum(tile, "mem")


def gap_weights(pair_list, pair_count, band_weight, cov_scale):
    slots = pair_list.shape[0]
    blocks_all = lax.axis_size("space")
    gap = (pair_list[:, 1] - pair_list[:, 0]) % blocks_all
    living = (jnp.arange(slots, dtype=jnp.int32) < pair_count[0]).astype(jnp.float32)
    bands = jnp.arange(NBANDS, dtype=jnp.int32)
    band_now = jnp.sum(
        jnp.where(pair_list[:, 2][:, None] == bands[None, :], band_weight[None, :], 0.0), axis=1
    )
    slot_weight = cov_scale[0] * band_now * living / (MEMBERS - 1)
    gaps = jnp.arange(REACH_DEV + 1, dtype=jnp.int32)
    return jnp.sum(jnp.where(gap[:, None] == gaps[None, :], slot_weight[:, None], 0.0), axis=0)


def by_collectives(perturb, pair_list, pair_count, band_weight, cov_scale, target, first_guess):
    w = gap_weights(pair_list, pair_count, band_weight, cov_scale)
    w_next = shifted(w, "space", -1)
    p0 = lax.all_to_all(perturb, "space", split_axis=1, concat_axis=0, tiled=True)
    p1 = shifted(p0, "space", -1)
    p3 = shifted(p0, "space", -3)
    x0 = first_guess
    t0 = mm(p0, p0, 0, 0) * w[0]
    t1 = mm(p0, p1, 0, 0) * w[1]
    t3 = mm(p0, p3, 0, 0) * w[3]
    t2 = mm(p1, p3, 0, 0) * w_next[2]
    t0, t1, t2, t3 = (member_sum(t) for t in (t0, t1, t2, t3))
    for sweep in range(ITERS):
        x1 = shifted(x0, "space", -1)
        x3 = shifted(x0, "space", -3)
        back1 = shifted(mm(t1, x0, 0, 0) + mm(t2, x3, 1, 0), "space", 1)
        back3 = shifted(mm(t3, x0, 0, 0) + mm(t2, x1, 0, 0), "space", 3)
        own = mm(t0, x0, 1, 0) + mm(t1, x1, 1, 0) + mm(t3, x3, 1, 0)
        x0 = x0 + 0.5 * (target - x0 - (own + back1 + back3))
    return x0

GROUP = REACH_DEV + 1
NEAR = 2 * REACH_DEV + 1
PLANES = 4


def split(value):
    high = value.astype(jnp.bfloat16)
    return high, (value - high.astype(jnp.float32)).astype(jnp.bfloat16)


def dot(a, b, ca, cb):
    return lax.dot_general(a, b, (((ca,), (cb,)), ((), ())), preferred_element_type=jnp.float32)


class Mover:
    def __init__(self, send_sem, recv_sem, local_sem):
        self.send_sem, self.recv_sem, self.local_sem = send_sem, recv_sem, local_sem
        self.used = 0
        self.local = 0
        self.open = []

    def reserve(self, number):
        first = self.used
        self.used += number
        return first

    def make(self, source, target, device, send, recv):
        return pltpu.make_async_remote_copy(
            src_ref=source, dst_ref=target,
            send_sem=self.send_sem.at[send], recv_sem=self.recv_sem.at[recv],
            device_id=device, device_id_type=pl.DeviceIdType.MESH,
        )

    def to(self, source, target, device, send=None, recv=None):
        if send is None:
            send = recv = self.reserve(1)
        copy = self.make(source, target, device, send, recv)
        copy.start()
        self.open.append(copy)
        return copy

    def here(self, source, target):
        copy = pltpu.make_async_copy(source, target, self.local_sem.at[self.local])
        self.local += 1
        copy.start()
        return copy


def kernel(perturb, table, guess, target, out, gc, gb, chi, clo, bhi, blo, part, tile_hi, tile_lo,
           tabs, xb, tb, halo, xs, acc, px, ret_in, ahead, final, send_sem, recv_sem, local_sem):
    space = lax.axis_index("space")
    mem = lax.axis_index("mem")
    k = space // GROUP
    j = space % GROUP
    rows = perturb.shape[0]
    half = rows // 2
    cols = xb.shape[2]
    B = BLOCK
    wide = REACH_DEV * B
    inner = GROUP * B
    each = 2 * GROUP * rows

    def plane(p):
        return (p * GROUP + j, mem)

    def chip(q):
        return (k * GROUP + q, mem)

    xn = chip(j + 1 - 2 * (j % 2))
    yn = chip((j + 2) % GROUP)
    partner = (space, 1 - mem)
    before = plane((k + PLANES - 1) % PLANES)
    after = plane((k + 1) % PLANES)

    barrier = pltpu.get_barrier_semaphore()
    greeted = [plane((k + r) % PLANES) for r in range(1, PLANES)]
    greeted += [chip((j + q) % GROUP) for q in range(1, GROUP)] + [partner]
    for device in greeted:
        pl.semaphore_signal(barrier, inc=1, device_id=device, device_id_type=pl.DeviceIdType.MESH)

    move = Mover(send_sem, recv_sem, local_sem)

    def at(block, size):
        return pl.ds(pl.multiple_of(block * B, B), size * B)

    def piece(q):
        return pl.ds(pl.multiple_of(q * cols, cols), cols)

    def pieces(p, slot):
        first = p * GROUP
        after_first = ((p + 1) % PLANES) * GROUP
        return (
            (perturb.at[:, at(first + 1, REACH_DEV)], gc.at[slot, 0, 0, :, pl.ds(0, wide)]),
            (perturb.at[:, at(after_first, REACH_DEV)], gc.at[slot, 0, 0, :, pl.ds(wide, wide)]),
            (perturb.at[:, at(first, 1)], gb.at[0, 0, slot]),
        )

    own_here = [move.here(*pair) for pair in pieces(k, 0)]
    x_here = move.here(guess.at[:, piece(j)], xb.at[j])
    t_here = move.here(target.at[:, piece(j)], tb.at[j])
    tab_here = move.here(table, tabs.at[j])
    pl.semaphore_wait(barrier, len(greeted))

    zsem = move.reserve(3 * PLANES)
    other_half = 2 - 2 * (k // 2)
    late = 2 + (k + k // 2 + 1) % 2
    routes = ((k + 1 - 2 * (k % 2), 1), (other_half, late), (other_half + 1, late))

    def exchange(which):
        for n, (p, slot) in enumerate(routes):
            for m in which:
                source, place = pieces(p, slot)[m]
                move.to(source, place, plane(p), zsem + 3 * n + m, zsem + 3 * slot + m)

    def from_plane(slot, which):
        for m in which:
            place = pieces(k, slot)[m][1]
            move.make(place, place, before, zsem, zsem + 3 * slot + m).wait_recv()

    exchange((0, 1))
    for copy in own_here:
        copy.wait()

    class Gather:
        def __init__(self, buffer, cut):
            self.buffer, self.cut = buffer, cut

        def own(self):
            source = self.buffer.at[0, 0]
            self.cx = move.to(source, self.buffer.at[1, 0], xn)
            self.cy = move.to(source, self.buffer.at[2, 0], yn)
            self.done = [move.to(source, self.buffer.at[0, 1], partner)]

        def over(self, q):
            self.done.append(move.to(self.buffer.at[q, 0], self.buffer.at[q, 1], partner))

        def relay(self):
            low, high = pl.ds(0, self.cut), pl.ds(self.cut, self.cut)
            self.cx.wait_recv()
            first = move.to(self.buffer.at[1, 0, low], self.buffer.at[3, 0, low], yn)
            self.over(1)
            self.cy.wait_recv()
            second = move.to(self.buffer.at[2, 0, high], self.buffer.at[3, 0, high], xn)
            self.over(2)
            self.halves = (first, second)

        def corner(self):
            for copy in self.halves:
                copy.wait_recv()
            self.over(3)

        def ready(self):
            for copy in self.done:
                copy.wait_recv()

    cross = [Gather(gc.at[r], half) for r in range(PLANES)]
    edge = Gather(gb, PLANES // 2)
    cross[0].own()
    tab_here.wait()
    tab_copies = [move.to(tabs.at[j], tabs.at[j], chip((j + q) % GROUP)) for q in range(1, GROUP)]

    def share(source, blocks):
        copies = []
        for q in range(1, GROUP):
            there = (j + q) % GROUP
            copies.append(move.to(source.at[:, piece(there)], blocks.at[j], chip(there)))
        return copies

    x_copies = share(guess, xb)
    exchange((2,))

    def weight(a, d):
        return tabs[a, d : d + 1]

    def pair(span, n, first, size):
        own = pl.ds(pl.multiple_of(n * B, B), B)
        row = pl.ds(pl.multiple_of((n + first) * B, B), size * B)
        left = jnp.concatenate([chi[span, own], chi[span, own], clo[span, own]], 0)
        right = jnp.concatenate([chi[span, row], clo[span, row], chi[span, row]], 0)
        return dot(left, right, 0, 0)

    def members(r):
        span = pl.ds(r * each, each)
        chi[span], clo[span] = split(gc[r].reshape(each, 2 * wide))
        return span

    def products(r):
        span = members(r)

        def step(n, carry):
            value = pair(span, n, 0, GROUP)
            part[n] = value if r == 0 else part[n] + value
            return carry

        lax.fori_loop(0, REACH_DEV, step, 0)

    def finish(span, a, first, size):
        value = pair(span, a - 1, first, size) + part[a - 1, :, pl.ds(first * B, size * B)]
        for d in range(size):
            now = value[:, d * B : (d + 1) * B] * weight(a, first + d)
            there = pl.ds((first + d) * B, B)
            tile_hi[a, :, there], tile_lo[a, :, there] = split(now)

    def edge_products():
        for r in range(PLANES):
            span = pl.ds(r * each, each)
            bhi[span], blo[span] = split(gb[:, :, r].reshape(each, B))
        left = jnp.concatenate([bhi[...], bhi[...], blo[...]], 0)
        right = jnp.concatenate([bhi[...], blo[...], bhi[...]], 0)
        now = dot(left, right, 0, 0) * weight(0, 0)
        tile_hi[0, :, :B], tile_lo[0, :, :B] = split(now)
        for d in range(1, GROUP):
            there = pl.ds((d - 1) * B, B)
            right = jnp.concatenate([chi[:, there], clo[:, there], chi[:, there]], 0)
            now = dot(left, right, 0, 0) * weight(0, d)
            place = pl.ds(d * B, B)
            tile_hi[0, :, place], tile_lo[0, :, place] = split(now)

    def times(high, low, x, side):
        both = dot(high, x, side, 0)
        return both[:, :cols] + both[:, cols:] + dot(low, x[:, :cols], side, 0)

    def block(n, size=1):
        return pl.ds(n * B, size * B)

    def set_x(n, value):
        xs[block(n), :cols], xs[block(n), cols:] = split(value)

    def forward(a, d, size):
        span = pl.ds(d * B, size * B)
        return times(tile_hi[a, :, span], tile_lo[a, :, span], xs[block(a + d, size)], 1)

    def down(a, first, size):
        span = pl.ds(first * B, size * B)
        return times(tile_hi[a, :, span], tile_lo[a, :, span], xs[block(a)], 0)

    def outgoing(sweep, ready):
        copies = {}
        for n in range(REACH_DEV - 1, -1, -1):
            a = n + 1
            ready(a)
            value = down(a, GROUP - a, a)
            if a == REACH_DEV:
                acc[sweep, block(GROUP, a)] = value
            else:
                acc[sweep, block(GROUP, a)] += value
            copies[n] = move.to(acc.at[sweep, block(GROUP + n)], ret_in.at[sweep, n], after)
        return copies

    def inside(sweep, a):
        acc[sweep, block(a + 1, REACH_DEV - a)] += down(a, 1, REACH_DEV - a)

    for slot in range(1, PLANES):
        from_plane(slot, (0, 1))
        cross[slot].own()
        cross[slot - 1].relay()
        if slot >= 2:
            cross[slot - 2].corner()
        if slot == 2:
            for copy in x_copies:
                copy.wait_recv()
            x_here.wait()
            halo_copy = move.to(xb.at[pl.ds(0, REACH_DEV)], halo, before)
    for slot in range(1, PLANES):
        from_plane(slot, (2,))
    edge.own()
    for n in range(GROUP):
        set_x(n, xb[n])
    cross[0].ready()
    products(0)
    cross[1].ready()
    products(1)
    cross[3].relay()
    cross[2].corner()
    cross[2].ready()
    products(2)
    edge.relay()
    t_copies = share(target, tb)
    halo_copy.wait_recv()
    for n in range(REACH_DEV):
        set_x(GROUP + n, halo[n])
    for copy in tab_copies:
        copy.wait_recv()
    cross[3].corner()
    cross[3].ready()
    last = members(PLANES - 1)
    for a in range(REACH_DEV, 0, -1):
        finish(last, a, GROUP - a, a)
    rets = outgoing(0, lambda a: None)
    for a in range(1, GROUP):
        finish(last, a, 0, GROUP - a)
    for a in range(1, GROUP):
        acc[0, block(a)] = forward(a, 0, GROUP)
    inside(0, 1)
    inside(0, 2)
    edge.corner()
    edge.ready()
    edge_products()
    inside(0, 0)
    acc[0, block(0)] = forward(0, 0, GROUP)
    for copy in t_copies:
        copy.wait_recv()
    t_here.wait()

    aheads = []
    for n in range(GROUP):
        px[n] = xb[n] + 0.5 * (tb[n] - xb[n] - acc[0, block(n)])
        if n < REACH_DEV:
            aheads.append(move.to(px.at[n], ahead.at[n], before))
    set_x(REACH_DEV, px[REACH_DEV])
    final[REACH_DEV] = px[REACH_DEV]

    def settle(n):
        if n < REACH_DEV:
            rets[n].wait_recv()
            now = px[n] - 0.5 * ret_in[0, n]
            set_x(n, now)
            final[n] = now

    rets_last = outgoing(1, settle)
    settle(0)
    for a in range(GROUP):
        acc[1, block(a)] = forward(a, 0, GROUP - a)
    for a in range(REACH_DEV):
        inside(1, a)

    base = move.reserve(GROUP)
    here_sem = local_sem.at[move.local]

    def leave(n, source):
        return move.make(final.at[n], out.at[:, piece(j)], chip(n), base + n, base + source)

    def stay(n):
        return pltpu.make_async_copy(final.at[n], out.at[:, piece(j)], here_sem)

    def put(n):
        change = acc[1, block(n)]
        if n < REACH_DEV:
            rets_last[n].wait_recv()
            change = change + ret_in[1, n]
        final[n] = final[n] + 0.5 * (tb[n] - final[n] - change)

        @pl.when(j != n)
        def _():
            leave(n, j).start()

        @pl.when(j == n)
        def _():
            stay(n).start()

    for n in range(REACH_DEV):
        aheads[n].wait_recv()
        set_x(GROUP + n, ahead[n] - 0.5 * acc[0, block(GROUP + n)])
        for a in range(n + 1, GROUP):
            acc[1, block(a)] += forward(a, GROUP + n - a, 1)
    for n in (3, 2, 1, 0):
        put(n)
    for n in range(GROUP):
        @pl.when(j != n)
        def _():
            leave(n, n).wait_send()
            leave(n, n).wait_recv()

        @pl.when(j == n)
        def _():
            stay(n).wait()
    for copy in move.open:
        copy.wait_send()


def in_one_kernel(perturb, pair_list, pair_count, band_weight, cov_scale, target, first_guess):
    w = gap_weights(pair_list, pair_count, band_weight, cov_scale)
    table = jnp.broadcast_to(jnp.pad(w, (0, 8 - w.shape[0]))[:, None], (8, BLOCK))
    rows = perturb.shape[0]
    cols = first_guess.shape[1] // GROUP
    members = 2 * GROUP * PLANES * rows
    f32, bf16 = jnp.float32, jnp.bfloat16
    sems = 112
    vmem = pl.BlockSpec(memory_space=pltpu.VMEM)
    anywhere = pl.BlockSpec(memory_space=pl.ANY)
    return pl.pallas_call(
        kernel,
        out_shape=jax.ShapeDtypeStruct(first_guess.shape, f32),
        in_specs=[anywhere, vmem, anywhere, anywhere],
        out_specs=vmem,
        scratch_shapes=[
            pltpu.VMEM((PLANES, GROUP, 2, rows, 2 * REACH_DEV * BLOCK), f32),
            pltpu.VMEM((GROUP, 2, PLANES, rows, BLOCK), f32),
            pltpu.VMEM((members, 2 * REACH_DEV * BLOCK), bf16),
            pltpu.VMEM((members, 2 * REACH_DEV * BLOCK), bf16),
            pltpu.VMEM((members, BLOCK), bf16),
            pltpu.VMEM((members, BLOCK), bf16),
            pltpu.VMEM((REACH_DEV, BLOCK, GROUP * BLOCK), f32),
            pltpu.VMEM((GROUP, BLOCK, GROUP * BLOCK), bf16),
            pltpu.VMEM((GROUP, BLOCK, GROUP * BLOCK), bf16),
            pltpu.VMEM((GROUP, 8, BLOCK), f32),
            pltpu.VMEM((GROUP, BLOCK, cols), f32),
            pltpu.VMEM((GROUP, BLOCK, cols), f32),
            pltpu.VMEM((REACH_DEV, BLOCK, cols), f32),
            pltpu.VMEM((NEAR * BLOCK, 2 * cols), bf16),
            pltpu.VMEM((2, NEAR * BLOCK, cols), f32),
            pltpu.VMEM((GROUP, BLOCK, cols), f32),
            pltpu.VMEM((2, REACH_DEV, BLOCK, cols), f32),
            pltpu.VMEM((REACH_DEV, BLOCK, cols), f32),
            pltpu.VMEM((GROUP, BLOCK, cols), f32),
            pltpu.SemaphoreType.DMA((sems,)),
            pltpu.SemaphoreType.DMA((sems,)),
            pltpu.SemaphoreType.DMA((8,)),
        ],
        compiler_params=pltpu.CompilerParams(
            collective_id=0, has_side_effects=True, vmem_limit_bytes=56 * 1024 * 1024
        ),
    )(perturb, table, first_guess, target)


def fits(perturb, field):
    return (
        lax.axis_size("mem") == 2 and lax.axis_size("space") == PLANES * GROUP
        and perturb.shape[0] % 16 == 0 and field.shape[1] % (GROUP * 128) == 0
        and field.shape[0] == BLOCK
    )


def per_device(perturb, pair_list, pair_count, band_weight, cov_scale, target, first_guess):
    whole = in_one_kernel if fits(perturb, first_guess) else by_collectives
    return whole(perturb, pair_list, pair_count, band_weight, cov_scale, target, first_guess)


def solution(mesh):
    in_specs = (
        P(("space", "mem"), None),
        P("space", None),
        P("space"),
        P(),
        P(),
        P("space", "mem"),
        P("space", "mem"),
    )
    out_specs = P("space", "mem")
    return jax.shard_map(
        per_device, mesh=mesh, in_specs=in_specs, out_specs=out_specs, check_vma=False
    )
```

```python
import functools
import jax
import jax.numpy as jnp
from jax import lax
from jax.experimental import pallas as pl
from jax.experimental.pallas import tpu as pltpu
from jax.sharding import PartitionSpec as P

BLOCK = 256
MEMBERS = 1024
REACH_DEV = 3
NBANDS = 8
ITERS = 2


def shifted(array, axis, by):
    count = lax.axis_size(axis)
    return lax.ppermute(array, axis, [(i, (i + by) % count) for i in range(count)])


def mm(a, b, ca, cb):
    return lax.dot_general(
        a, b, (((ca,), (cb,)), ((), ())), precision=lax.Precision.HIGH,
        preferred_element_type=jnp.float32,
    )


def member_sum(tile):
    if lax.axis_size("mem") == 2:
        return tile + shifted(tile, "mem", 1)
    return lax.psum(tile, "mem")


def gap_weights(pair_list, pair_count, band_weight, cov_scale):
    slots = pair_list.shape[0]
    blocks_all = lax.axis_size("space")
    gap = (pair_list[:, 1] - pair_list[:, 0]) % blocks_all
    living = (jnp.arange(slots, dtype=jnp.int32) < pair_count[0]).astype(jnp.float32)
    bands = jnp.arange(NBANDS, dtype=jnp.int32)
    band_now = jnp.sum(
        jnp.where(pair_list[:, 2][:, None] == bands[None, :], band_weight[None, :], 0.0), axis=1
    )
    slot_weight = cov_scale[0] * band_now * living / (MEMBERS - 1)
    gaps = jnp.arange(REACH_DEV + 1, dtype=jnp.int32)
    return jnp.sum(jnp.where(gap[:, None] == gaps[None, :], slot_weight[:, None], 0.0), axis=0)


def by_collectives(perturb, pair_list, pair_count, band_weight, cov_scale, target, first_guess):
    w = gap_weights(pair_list, pair_count, band_weight, cov_scale)
    w_next = shifted(w, "space", -1)
    p0 = lax.all_to_all(perturb, "space", split_axis=1, concat_axis=0, tiled=True)
    p1 = shifted(p0, "space", -1)
    p3 = shifted(p0, "space", -3)
    x0 = first_guess
    t0 = mm(p0, p0, 0, 0) * w[0]
    t1 = mm(p0, p1, 0, 0) * w[1]
    t3 = mm(p0, p3, 0, 0) * w[3]
    t2 = mm(p1, p3, 0, 0) * w_next[2]
    t0, t1, t2, t3 = (member_sum(t) for t in (t0, t1, t2, t3))
    for sweep in range(ITERS):
        x1 = shifted(x0, "space", -1)
        x3 = shifted(x0, "space", -3)
        back1 = shifted(mm(t1, x0, 0, 0) + mm(t2, x3, 1, 0), "space", 1)
        back3 = shifted(mm(t3, x0, 0, 0) + mm(t2, x1, 0, 0), "space", 3)
        own = mm(t0, x0, 1, 0) + mm(t1, x1, 1, 0) + mm(t3, x3, 1, 0)
        x0 = x0 + 0.5 * (target - x0 - (own + back1 + back3))
    return x0

GROUP = REACH_DEV + 1
NEAR = 2 * REACH_DEV + 1
PLANES = 4


def split(value):
    high = value.astype(jnp.bfloat16)
    return high, (value - high.astype(jnp.float32)).astype(jnp.bfloat16)


def dot(a, b, ca, cb):
    return lax.dot_general(a, b, (((ca,), (cb,)), ((), ())), preferred_element_type=jnp.float32)


class Mover:
    def __init__(self, send_sem, recv_sem, local_sem):
        self.send_sem, self.recv_sem, self.local_sem = send_sem, recv_sem, local_sem
        self.used = 0
        self.local = 0
        self.open = []

    def reserve(self, number):
        first = self.used
        self.used += number
        return first

    def make(self, source, target, device, send, recv):
        return pltpu.make_async_remote_copy(
            src_ref=source, dst_ref=target,
            send_sem=self.send_sem.at[send], recv_sem=self.recv_sem.at[recv],
            device_id=device, device_id_type=pl.DeviceIdType.MESH,
        )

    def to(self, source, target, device, send=None, recv=None):
        if send is None:
            send = recv = self.reserve(1)
        copy = self.make(source, target, device, send, recv)
        copy.start()
        self.open.append(copy)
        return copy

    def here(self, source, target):
        copy = pltpu.make_async_copy(source, target, self.local_sem.at[self.local])
        self.local += 1
        copy.start()
        return copy


def kernel(perturb, table, guess, target, out, gc, gb, chi, clo, bhi, blo, part, tile_hi, tile_lo,
           tabs, xb, tb, halo, xs, acc, px, ret_in, ahead, final, via, send_sem, recv_sem, local_sem):
    space = lax.axis_index("space")
    mem = lax.axis_index("mem")
    k = space // GROUP
    j = space % GROUP
    rows = perturb.shape[0]
    half = rows // 2
    cols = xb.shape[2]
    B = BLOCK
    wide = REACH_DEV * B
    inner = GROUP * B
    each = 2 * GROUP * rows

    def plane(p):
        return (p * GROUP + j, mem)

    def chip(q):
        return (k * GROUP + q, mem)

    xn = chip(j + 1 - 2 * (j % 2))
    yn = chip((j + 2) % GROUP)
    partner = (space, 1 - mem)
    before = plane((k + PLANES - 1) % PLANES)
    after = plane((k + 1) % PLANES)

    barrier = pltpu.get_barrier_semaphore()
    greeted = [plane((k + r) % PLANES) for r in range(1, PLANES)]
    greeted += [chip((j + q) % GROUP) for q in range(1, GROUP)] + [partner]
    for device in greeted:
        pl.semaphore_signal(barrier, inc=1, device_id=device, device_id_type=pl.DeviceIdType.MESH)

    move = Mover(send_sem, recv_sem, local_sem)

    def at(block, size):
        return pl.ds(pl.multiple_of(block * B, B), size * B)

    def piece(q):
        return pl.ds(pl.multiple_of(q * cols, cols), cols)

    def pieces(p, slot):
        first = p * GROUP
        after_first = ((p + 1) % PLANES) * GROUP
        return (
            (perturb.at[:, at(first + 1, REACH_DEV)], gc.at[slot, 0, 0, :, pl.ds(0, wide)]),
            (perturb.at[:, at(after_first, REACH_DEV)], gc.at[slot, 0, 0, :, pl.ds(wide, wide)]),
            (perturb.at[:, at(first, 1)], gb.at[0, 0, slot]),
        )

    own_here = [move.here(*pair) for pair in pieces(k, 0)]
    x_here = move.here(guess.at[:, piece(j)], xb.at[j])
    t_here = move.here(target.at[:, piece(j)], tb.at[j])
    tab_here = move.here(table, tabs.at[j])
    pl.semaphore_wait(barrier, len(greeted))

    zsem = move.reserve(3 * PLANES)
    other_half = 2 - 2 * (k // 2)
    late = 2 + (k + k // 2 + 1) % 2
    routes = ((k + 1 - 2 * (k % 2), 1), (other_half, late), (other_half + 1, late))

    def exchange(which):
        for n, (p, slot) in enumerate(routes):
            for m in which:
                source, place = pieces(p, slot)[m]
                move.to(source, place, plane(p), zsem + 3 * n + m, zsem + 3 * slot + m)

    def from_plane(slot, which):
        for m in which:
            place = pieces(k, slot)[m][1]
            move.make(place, place, before, zsem, zsem + 3 * slot + m).wait_recv()

    exchange((0, 1))
    for copy in own_here:
        copy.wait()

    class Gather:
        def __init__(self, buffer, cut):
            self.buffer, self.cut = buffer, cut

        def own(self):
            source = self.buffer.at[0, 0]
            self.cx = move.to(source, self.buffer.at[1, 0], xn)
            self.cy = move.to(source, self.buffer.at[2, 0], yn)
            self.done = [move.to(source, self.buffer.at[0, 1], partner)]

        def over(self, q):
            self.done.append(move.to(self.buffer.at[q, 0], self.buffer.at[q, 1], partner))

        def relay(self):
            low, high = pl.ds(0, self.cut), pl.ds(self.cut, self.cut)
            self.cx.wait_recv()
            first = move.to(self.buffer.at[1, 0, low], self.buffer.at[3, 0, low], yn)
            self.over(1)
            self.cy.wait_recv()
            second = move.to(self.buffer.at[2, 0, high], self.buffer.at[3, 0, high], xn)
            self.over(2)
            self.halves = (first, second)

        def corner(self):
            for copy in self.halves:
                copy.wait_recv()
            self.over(3)

        def ready(self):
            for copy in self.done:
                copy.wait_recv()

    cross = [Gather(gc.at[r], half) for r in range(PLANES)]
    edge = Gather(gb, PLANES // 2)
    cross[0].own()
    tab_here.wait()
    tab_copies = [move.to(tabs.at[j], tabs.at[j], chip((j + q) % GROUP)) for q in range(1, GROUP)]

    jx = j + 1 - 2 * (j % 2)
    jy = (j + 2) % GROUP
    jd = (jx + 2) % GROUP
    top, bottom = pl.ds(0, B // 2), pl.ds(B // 2, B // 2)

    class Share:
        def __init__(self, source, blocks, via):
            self.blocks, self.via = blocks, via
            self.first = move.to(source.at[top, piece(jd)], via.at[0], xn)
            self.second = move.to(source.at[bottom, piece(jd)], via.at[1], yn)
            self.done = [move.to(source.at[:, piece(jx)], blocks.at[j], xn),
                         move.to(source.at[:, piece(jy)], blocks.at[j], yn)]

        def relay(self):
            self.first.wait_recv()
            self.done.append(move.to(self.via.at[0], self.blocks.at[jx, top], yn))
            self.second.wait_recv()
            self.done.append(move.to(self.via.at[1], self.blocks.at[jy, bottom], xn))

        def ready(self):
            for copy in self.done:
                copy.wait_recv()

    x_share = Share(guess, xb, via.at[0])
    exchange((2,))

    def weight(a, d):
        return tabs[a, d : d + 1]

    def pair(span, n, first, size):
        own = pl.ds(pl.multiple_of(n * B, B), B)
        row = pl.ds(pl.multiple_of((n + first) * B, B), size * B)
        left = jnp.concatenate([chi[span, own], chi[span, own], clo[span, own]], 0)
        right = jnp.concatenate([chi[span, row], clo[span, row], chi[span, row]], 0)
        return dot(left, right, 0, 0)

    def members(r):
        span = pl.ds(r * each, each)
        chi[span], clo[span] = split(gc[r].reshape(each, 2 * wide))
        return span

    def products(r):
        span = members(r)

        def step(n, carry):
            value = pair(span, n, 0, GROUP)
            part[n] = value if r == 0 else part[n] + value
            return carry

        lax.fori_loop(0, REACH_DEV, step, 0)

    def finish(span, a, first, size):
        value = pair(span, a - 1, first, size) + part[a - 1, :, pl.ds(first * B, size * B)]
        for d in range(size):
            now = value[:, d * B : (d + 1) * B] * weight(a, first + d)
            there = pl.ds((first + d) * B, B)
            tile_hi[a, :, there], tile_lo[a, :, there] = split(now)

    def edge_products():
        for r in range(PLANES):
            span = pl.ds(r * each, each)
            bhi[span], blo[span] = split(gb[:, :, r].reshape(each, B))
        left = jnp.concatenate([bhi[...], bhi[...], blo[...]], 0)
        right = jnp.concatenate([bhi[...], blo[...], bhi[...]], 0)
        now = dot(left, right, 0, 0) * weight(0, 0)
        tile_hi[0, :, :B], tile_lo[0, :, :B] = split(now)
        for d in range(1, GROUP):
            there = pl.ds((d - 1) * B, B)
            right = jnp.concatenate([chi[:, there], clo[:, there], chi[:, there]], 0)
            now = dot(left, right, 0, 0) * weight(0, d)
            place = pl.ds(d * B, B)
            tile_hi[0, :, place], tile_lo[0, :, place] = split(now)

    def times(high, low, x, side):
        both = dot(high, x, side, 0)
        return both[:, :cols] + both[:, cols:] + dot(low, x[:, :cols], side, 0)

    def block(n, size=1):
        return pl.ds(n * B, size * B)

    def set_x(n, value):
        xs[block(n), :cols], xs[block(n), cols:] = split(value)

    def forward(a, d, size):
        span = pl.ds(d * B, size * B)
        return times(tile_hi[a, :, span], tile_lo[a, :, span], xs[block(a + d, size)], 1)

    def down(a, first, size):
        span = pl.ds(first * B, size * B)
        return times(tile_hi[a, :, span], tile_lo[a, :, span], xs[block(a)], 0)

    def outgoing(sweep, ready):
        copies = {}
        for n in range(REACH_DEV - 1, -1, -1):
            a = n + 1
            ready(a)
            value = down(a, GROUP - a, a)
            if a == REACH_DEV:
                acc[sweep, block(GROUP, a)] = value
            else:
                acc[sweep, block(GROUP, a)] += value
            copies[n] = move.to(acc.at[sweep, block(GROUP + n)], ret_in.at[sweep, n], after)
        return copies

    def inside(sweep, a):
        acc[sweep, block(a + 1, REACH_DEV - a)] += down(a, 1, REACH_DEV - a)

    for slot in range(1, PLANES):
        from_plane(slot, (0, 1))
        cross[slot].own()
        cross[slot - 1].relay()
        if slot == 1:
            x_share.relay()
        if slot >= 2:
            cross[slot - 2].corner()
        if slot == 2:
            x_share.ready()
            x_here.wait()
            halo_copy = move.to(xb.at[pl.ds(0, REACH_DEV)], halo, before)
    for slot in range(1, PLANES):
        from_plane(slot, (2,))
    edge.own()
    for n in range(GROUP):
        set_x(n, xb[n])
    cross[0].ready()
    products(0)
    cross[1].ready()
    products(1)
    cross[3].relay()
    cross[2].corner()
    cross[2].ready()
    products(2)
    edge.relay()
    t_share = Share(target, tb, via.at[1])
    halo_copy.wait_recv()
    for n in range(REACH_DEV):
        set_x(GROUP + n, halo[n])
    for copy in tab_copies:
        copy.wait_recv()
    cross[3].corner()
    cross[3].ready()
    last = members(PLANES - 1)
    for a in range(REACH_DEV, 0, -1):
        finish(last, a, GROUP - a, a)
    rets = outgoing(0, lambda a: None)
    t_share.relay()
    for a in range(1, GROUP):
        finish(last, a, 0, GROUP - a)
    for a in range(1, GROUP):
        acc[0, block(a)] = forward(a, 0, GROUP)
    inside(0, 1)
    inside(0, 2)
    edge.corner()
    edge.ready()
    edge_products()
    inside(0, 0)
    acc[0, block(0)] = forward(0, 0, GROUP)
    t_share.ready()
    t_here.wait()

    aheads = []
    for n in range(GROUP):
        px[n] = xb[n] + 0.5 * (tb[n] - xb[n] - acc[0, block(n)])
        if n < REACH_DEV:
            aheads.append(move.to(px.at[n], ahead.at[n], before))
    set_x(REACH_DEV, px[REACH_DEV])
    final[REACH_DEV] = px[REACH_DEV]

    def settle(n):
        if n < REACH_DEV:
            rets[n].wait_recv()
            now = px[n] - 0.5 * ret_in[0, n]
            set_x(n, now)
            final[n] = now

    rets_last = outgoing(1, settle)
    settle(0)
    for a in range(GROUP):
        acc[1, block(a)] = forward(a, 0, GROUP - a)
    for a in range(REACH_DEV):
        inside(1, a)

    base = move.reserve(GROUP)
    here_sem = local_sem.at[move.local]

    def leave(n, source):
        return move.make(final.at[n], out.at[:, piece(j)], chip(n), base + n, base + source)

    def stay(n):
        return pltpu.make_async_copy(final.at[n], out.at[:, piece(j)], here_sem)

    def put(n):
        change = acc[1, block(n)]
        if n < REACH_DEV:
            rets_last[n].wait_recv()
            change = change + ret_in[1, n]
        final[n] = final[n] + 0.5 * (tb[n] - final[n] - change)

        @pl.when(j != n)
        def _():
            leave(n, j).start()

        @pl.when(j == n)
        def _():
            stay(n).start()

    for n in range(REACH_DEV):
        aheads[n].wait_recv()
        set_x(GROUP + n, ahead[n] - 0.5 * acc[0, block(GROUP + n)])
        for a in range(n + 1, GROUP):
            acc[1, block(a)] += forward(a, GROUP + n - a, 1)
    for n in (3, 2, 1, 0):
        put(n)
    for n in range(GROUP):
        @pl.when(j != n)
        def _():
            leave(n, n).wait_send()
            leave(n, n).wait_recv()

        @pl.when(j == n)
        def _():
            stay(n).wait()
    for copy in move.open:
        copy.wait_send()


def in_one_kernel(perturb, pair_list, pair_count, band_weight, cov_scale, target, first_guess):
    w = gap_weights(pair_list, pair_count, band_weight, cov_scale)
    table = jnp.broadcast_to(jnp.pad(w, (0, 8 - w.shape[0]))[:, None], (8, BLOCK))
    rows = perturb.shape[0]
    cols = first_guess.shape[1] // GROUP
    members = 2 * GROUP * PLANES * rows
    f32, bf16 = jnp.float32, jnp.bfloat16
    sems = 112
    vmem = pl.BlockSpec(memory_space=pltpu.VMEM)
    anywhere = pl.BlockSpec(memory_space=pl.ANY)
    return pl.pallas_call(
        kernel,
        out_shape=jax.ShapeDtypeStruct(first_guess.shape, f32),
        in_specs=[anywhere, vmem, anywhere, anywhere],
        out_specs=vmem,
        scratch_shapes=[
            pltpu.VMEM((PLANES, GROUP, 2, rows, 2 * REACH_DEV * BLOCK), f32),
            pltpu.VMEM((GROUP, 2, PLANES, rows, BLOCK), f32),
            pltpu.VMEM((members, 2 * REACH_DEV * BLOCK), bf16),
            pltpu.VMEM((members, 2 * REACH_DEV * BLOCK), bf16),
            pltpu.VMEM((members, BLOCK), bf16),
            pltpu.VMEM((members, BLOCK), bf16),
            pltpu.VMEM((REACH_DEV, BLOCK, GROUP * BLOCK), f32),
            pltpu.VMEM((GROUP, BLOCK, GROUP * BLOCK), bf16),
            pltpu.VMEM((GROUP, BLOCK, GROUP * BLOCK), bf16),
            pltpu.VMEM((GROUP, 8, BLOCK), f32),
            pltpu.VMEM((GROUP, BLOCK, cols), f32),
            pltpu.VMEM((GROUP, BLOCK, cols), f32),
            pltpu.VMEM((REACH_DEV, BLOCK, cols), f32),
            pltpu.VMEM((NEAR * BLOCK, 2 * cols), bf16),
            pltpu.VMEM((2, NEAR * BLOCK, cols), f32),
            pltpu.VMEM((GROUP, BLOCK, cols), f32),
            pltpu.VMEM((2, REACH_DEV, BLOCK, cols), f32),
            pltpu.VMEM((REACH_DEV, BLOCK, cols), f32),
            pltpu.VMEM((GROUP, BLOCK, cols), f32),
            pltpu.VMEM((2, 2, BLOCK // 2, cols), f32),
            pltpu.SemaphoreType.DMA((sems,)),
            pltpu.SemaphoreType.DMA((sems,)),
            pltpu.SemaphoreType.DMA((8,)),
        ],
        compiler_params=pltpu.CompilerParams(
            collective_id=0, has_side_effects=True, vmem_limit_bytes=56 * 1024 * 1024
        ),
    )(perturb, table, first_guess, target)


def fits(perturb, field):
    return (
        lax.axis_size("mem") == 2 and lax.axis_size("space") == PLANES * GROUP
        and perturb.shape[0] % 16 == 0 and field.shape[1] % (GROUP * 128) == 0
        and field.shape[0] == BLOCK
    )


def per_device(perturb, pair_list, pair_count, band_weight, cov_scale, target, first_guess):
    whole = in_one_kernel if fits(perturb, first_guess) else by_collectives
    return whole(perturb, pair_list, pair_count, band_weight, cov_scale, target, first_guess)


def solution(mesh):
    in_specs = (
        P(("space", "mem"), None),
        P("space", None),
        P("space"),
        P(),
        P(),
        P("space", "mem"),
        P("space", "mem"),
    )
    out_specs = P("space", "mem")
    return jax.shard_map(
        per_device, mesh=mesh, in_specs=in_specs, out_specs=out_specs, check_vma=False
    )
```

```python
import functools
import jax
import jax.numpy as jnp
from jax import lax
from jax.experimental import pallas as pl
from jax.experimental.pallas import tpu as pltpu
from jax.sharding import PartitionSpec as P

BLOCK = 256
MEMBERS = 1024
REACH_DEV = 3
NBANDS = 8
ITERS = 2


def shifted(array, axis, by):
    count = lax.axis_size(axis)
    return lax.ppermute(array, axis, [(i, (i + by) % count) for i in range(count)])


def mm(a, b, ca, cb):
    return lax.dot_general(
        a, b, (((ca,), (cb,)), ((), ())), precision=lax.Precision.HIGH,
        preferred_element_type=jnp.float32,
    )


def member_sum(tile):
    if lax.axis_size("mem") == 2:
        return tile + shifted(tile, "mem", 1)
    return lax.psum(tile, "mem")


def gap_weights(pair_list, pair_count, band_weight, cov_scale):
    slots = pair_list.shape[0]
    blocks_all = lax.axis_size("space")
    gap = (pair_list[:, 1] - pair_list[:, 0]) % blocks_all
    living = (jnp.arange(slots, dtype=jnp.int32) < pair_count[0]).astype(jnp.float32)
    bands = jnp.arange(NBANDS, dtype=jnp.int32)
    band_now = jnp.sum(
        jnp.where(pair_list[:, 2][:, None] == bands[None, :], band_weight[None, :], 0.0), axis=1
    )
    slot_weight = cov_scale[0] * band_now * living / (MEMBERS - 1)
    gaps = jnp.arange(REACH_DEV + 1, dtype=jnp.int32)
    return jnp.sum(jnp.where(gap[:, None] == gaps[None, :], slot_weight[:, None], 0.0), axis=0)


def by_collectives(perturb, pair_list, pair_count, band_weight, cov_scale, target, first_guess):
    w = gap_weights(pair_list, pair_count, band_weight, cov_scale)
    w_next = shifted(w, "space", -1)
    p0 = lax.all_to_all(perturb, "space", split_axis=1, concat_axis=0, tiled=True)
    p1 = shifted(p0, "space", -1)
    p3 = shifted(p0, "space", -3)
    x0 = first_guess
    t0 = mm(p0, p0, 0, 0) * w[0]
    t1 = mm(p0, p1, 0, 0) * w[1]
    t3 = mm(p0, p3, 0, 0) * w[3]
    t2 = mm(p1, p3, 0, 0) * w_next[2]
    t0, t1, t2, t3 = (member_sum(t) for t in (t0, t1, t2, t3))
    for sweep in range(ITERS):
        x1 = shifted(x0, "space", -1)
        x3 = shifted(x0, "space", -3)
        back1 = shifted(mm(t1, x0, 0, 0) + mm(t2, x3, 1, 0), "space", 1)
        back3 = shifted(mm(t3, x0, 0, 0) + mm(t2, x1, 0, 0), "space", 3)
        own = mm(t0, x0, 1, 0) + mm(t1, x1, 1, 0) + mm(t3, x3, 1, 0)
        x0 = x0 + 0.5 * (target - x0 - (own + back1 + back3))
    return x0

GROUP = REACH_DEV + 1
NEAR = 2 * REACH_DEV + 1
PLANES = 4


def split(value):
    high = value.astype(jnp.bfloat16)
    return high, (value - high.astype(jnp.float32)).astype(jnp.bfloat16)


def dot(a, b, ca, cb):
    return lax.dot_general(a, b, (((ca,), (cb,)), ((), ())), preferred_element_type=jnp.float32)


class Mover:
    def __init__(self, send_sem, recv_sem, local_sem):
        self.send_sem, self.recv_sem, self.local_sem = send_sem, recv_sem, local_sem
        self.used = 0
        self.local = 0
        self.open = []

    def reserve(self, number):
        first = self.used
        self.used += number
        return first

    def make(self, source, target, device, send, recv):
        return pltpu.make_async_remote_copy(
            src_ref=source, dst_ref=target,
            send_sem=self.send_sem.at[send], recv_sem=self.recv_sem.at[recv],
            device_id=device, device_id_type=pl.DeviceIdType.MESH,
        )

    def to(self, source, target, device, send=None, recv=None):
        if send is None:
            send = recv = self.reserve(1)
        copy = self.make(source, target, device, send, recv)
        copy.start()
        self.open.append(copy)
        return copy

    def here(self, source, target):
        copy = pltpu.make_async_copy(source, target, self.local_sem.at[self.local])
        self.local += 1
        copy.start()
        return copy


def kernel(perturb, table, guess, target, out, gc, gb, chi, clo, bhi, blo, part, tile_hi, tile_lo,
           tabs, xb, tb, halo, xs, acc, px, ret_in, ahead, final, via, send_sem, recv_sem, local_sem):
    space = lax.axis_index("space")
    mem = lax.axis_index("mem")
    k = space // GROUP
    j = space % GROUP
    rows = perturb.shape[0]
    half = rows // 2
    cols = xb.shape[2]
    B = BLOCK
    wide = REACH_DEV * B
    inner = GROUP * B
    each = 2 * GROUP * rows

    def plane(p):
        return (p * GROUP + j, mem)

    def chip(q):
        return (k * GROUP + q, mem)

    xn = chip(j + 1 - 2 * (j % 2))
    yn = chip((j + 2) % GROUP)
    partner = (space, 1 - mem)
    before = plane((k + PLANES - 1) % PLANES)
    after = plane((k + 1) % PLANES)

    barrier = pltpu.get_barrier_semaphore()
    greeted = [plane((k + r) % PLANES) for r in range(1, PLANES)]
    greeted += [chip((j + q) % GROUP) for q in range(1, GROUP)] + [partner]
    for device in greeted:
        pl.semaphore_signal(barrier, inc=1, device_id=device, device_id_type=pl.DeviceIdType.MESH)

    move = Mover(send_sem, recv_sem, local_sem)

    def at(block, size):
        return pl.ds(pl.multiple_of(block * B, B), size * B)

    def piece(q):
        return pl.ds(pl.multiple_of(q * cols, cols), cols)

    def pieces(p, slot):
        first = p * GROUP
        after_first = ((p + 1) % PLANES) * GROUP
        return (
            (perturb.at[:, at(first + 1, REACH_DEV)], gc.at[slot, 0, 0, :, pl.ds(0, wide)]),
            (perturb.at[:, at(after_first, REACH_DEV)], gc.at[slot, 0, 0, :, pl.ds(wide, wide)]),
            (perturb.at[:, at(first, 1)], gb.at[0, 0, slot]),
        )

    own_here = [move.here(*pair) for pair in pieces(k, 0)]
    x_here = move.here(guess.at[:, piece(j)], xb.at[j])
    t_here = move.here(target.at[:, piece(j)], tb.at[j])
    tab_here = move.here(table, tabs.at[j])
    pl.semaphore_wait(barrier, len(greeted))

    zsem = move.reserve(3 * PLANES)
    other_half = 2 - 2 * (k // 2)
    late = 2 + (k + k // 2 + 1) % 2
    routes = ((k + 1 - 2 * (k % 2), 1), (other_half, late), (other_half + 1, late))

    def exchange(which):
        for n, (p, slot) in enumerate(routes):
            for m in which:
                source, place = pieces(p, slot)[m]
                move.to(source, place, plane(p), zsem + 3 * n + m, zsem + 3 * slot + m)

    def from_plane(slot, which):
        for m in which:
            place = pieces(k, slot)[m][1]
            move.make(place, place, before, zsem, zsem + 3 * slot + m).wait_recv()

    exchange((0, 1))
    for copy in own_here:
        copy.wait()

    class Gather:
        def __init__(self, buffer, cut):
            self.buffer, self.cut = buffer, cut

        def own(self):
            source = self.buffer.at[0, 0]
            self.cx = move.to(source, self.buffer.at[1, 0], xn)
            self.cy = move.to(source, self.buffer.at[2, 0], yn)
            self.done = [move.to(source, self.buffer.at[0, 1], partner)]

        def over(self, q):
            self.done.append(move.to(self.buffer.at[q, 0], self.buffer.at[q, 1], partner))

        def relay(self):
            low, high = pl.ds(0, self.cut), pl.ds(self.cut, self.cut)
            self.cx.wait_recv()
            first = move.to(self.buffer.at[1, 0, low], self.buffer.at[3, 0, low], yn)
            self.over(1)
            self.cy.wait_recv()
            second = move.to(self.buffer.at[2, 0, high], self.buffer.at[3, 0, high], xn)
            self.over(2)
            self.halves = (first, second)

        def corner(self):
            for copy in self.halves:
                copy.wait_recv()
            self.over(3)

        def ready(self):
            for copy in self.done:
                copy.wait_recv()

    cross = [Gather(gc.at[r], half) for r in range(PLANES)]
    edge = Gather(gb, PLANES // 2)
    cross[0].own()
    tab_here.wait()
    tab_copies = [move.to(tabs.at[j], tabs.at[j], chip((j + q) % GROUP)) for q in range(1, GROUP)]

    jx = j + 1 - 2 * (j % 2)
    jy = (j + 2) % GROUP
    jd = (jx + 2) % GROUP
    top, bottom = pl.ds(0, B // 2), pl.ds(B // 2, B // 2)

    class Share:
        def __init__(self, source, blocks, via):
            self.blocks, self.via = blocks, via
            self.first = move.to(source.at[top, piece(jd)], via.at[0], xn)
            self.second = move.to(source.at[bottom, piece(jd)], via.at[1], yn)
            self.done = [move.to(source.at[:, piece(jx)], blocks.at[j], xn),
                         move.to(source.at[:, piece(jy)], blocks.at[j], yn)]

        def relay(self):
            self.first.wait_recv()
            self.done.append(move.to(self.via.at[0], self.blocks.at[jx, top], yn))
            self.second.wait_recv()
            self.done.append(move.to(self.via.at[1], self.blocks.at[jy, bottom], xn))

        def ready(self):
            for copy in self.done:
                copy.wait_recv()

    x_share = Share(guess, xb, via.at[0])
    exchange((2,))

    def weight(a, d):
        return tabs[a, d : d + 1]

    def pair(span, n, first, size):
        own = pl.ds(pl.multiple_of(n * B, B), B)
        row = pl.ds(pl.multiple_of((n + first) * B, B), size * B)
        left = jnp.concatenate([chi[span, own], chi[span, own], clo[span, own]], 0)
        right = jnp.concatenate([chi[span, row], clo[span, row], chi[span, row]], 0)
        return dot(left, right, 0, 0)

    def members(r):
        span = pl.ds(r * each, each)
        chi[span], clo[span] = split(gc[r].reshape(each, 2 * wide))
        return span

    def products(r):
        span = members(r)

        def step(n, carry):
            value = pair(span, n, 0, GROUP)
            part[n] = value if r == 0 else part[n] + value
            return carry

        lax.fori_loop(0, REACH_DEV, step, 0)

    def finish(span, a, first, size):
        value = pair(span, a - 1, first, size) + part[a - 1, :, pl.ds(first * B, size * B)]
        for d in range(size):
            now = value[:, d * B : (d + 1) * B] * weight(a, first + d)
            there = pl.ds((first + d) * B, B)
            tile_hi[a, :, there], tile_lo[a, :, there] = split(now)

    def edge_products():
        for r in range(PLANES):
            span = pl.ds(r * each, each)
            bhi[span], blo[span] = split(gb[:, :, r].reshape(each, B))
        left = jnp.concatenate([bhi[...], bhi[...], blo[...]], 0)
        right = jnp.concatenate([bhi[...], blo[...], bhi[...]], 0)
        now = dot(left, right, 0, 0) * weight(0, 0)
        tile_hi[0, :, :B], tile_lo[0, :, :B] = split(now)
        for d in range(1, GROUP):
            there = pl.ds((d - 1) * B, B)
            right = jnp.concatenate([chi[:, there], clo[:, there], chi[:, there]], 0)
            now = dot(left, right, 0, 0) * weight(0, d)
            place = pl.ds(d * B, B)
            tile_hi[0, :, place], tile_lo[0, :, place] = split(now)

    def times(high, low, x, side):
        both = dot(high, x, side, 0)
        return both[:, :cols] + both[:, cols:] + dot(low, x[:, :cols], side, 0)

    def block(n, size=1):
        return pl.ds(n * B, size * B)

    def set_x(n, value):
        xs[block(n), :cols], xs[block(n), cols:] = split(value)

    def forward(a, d, size):
        span = pl.ds(d * B, size * B)
        return times(tile_hi[a, :, span], tile_lo[a, :, span], xs[block(a + d, size)], 1)

    def down(a, first, size):
        span = pl.ds(first * B, size * B)
        return times(tile_hi[a, :, span], tile_lo[a, :, span], xs[block(a)], 0)

    def outgoing(sweep, ready):
        copies = {}
        for n in range(REACH_DEV - 1, -1, -1):
            a = n + 1
            ready(a)
            value = down(a, GROUP - a, a)
            if a == REACH_DEV:
                acc[sweep, block(GROUP, a)] = value
            else:
                acc[sweep, block(GROUP, a)] += value
            copies[n] = move.to(acc.at[sweep, block(GROUP + n)], ret_in.at[sweep, n], after)
        return copies

    def inside(sweep, a):
        acc[sweep, block(a + 1, REACH_DEV - a)] += down(a, 1, REACH_DEV - a)

    for slot in range(1, PLANES):
        from_plane(slot, (0, 1))
        cross[slot].own()
        cross[slot - 1].relay()
        if slot == 1:
            x_share.relay()
            t_share = Share(target, tb, via.at[1])
        if slot >= 2:
            cross[slot - 2].corner()
        if slot == 2:
            t_share.relay()
        if slot == 3:
            x_share.ready()
            x_here.wait()
            halo_copy = move.to(xb.at[pl.ds(0, REACH_DEV)], halo, before)
    for slot in range(1, PLANES):
        from_plane(slot, (2,))
    edge.own()
    for n in range(GROUP):
        set_x(n, xb[n])
    cross[0].ready()
    products(0)
    cross[1].ready()
    products(1)
    cross[3].relay()
    cross[2].corner()
    cross[2].ready()
    products(2)
    edge.relay()
    halo_copy.wait_recv()
    for n in range(REACH_DEV):
        set_x(GROUP + n, halo[n])
    for copy in tab_copies:
        copy.wait_recv()
    cross[3].corner()
    cross[3].ready()
    last = members(PLANES - 1)
    for a in range(REACH_DEV, 0, -1):
        finish(last, a, GROUP - a, a)
    rets = outgoing(0, lambda a: None)
    for a in range(1, GROUP):
        finish(last, a, 0, GROUP - a)
    for a in range(1, GROUP):
        acc[0, block(a)] = forward(a, 0, GROUP)
    inside(0, 1)
    inside(0, 2)
    edge.corner()
    edge.ready()
    edge_products()
    inside(0, 0)
    acc[0, block(0)] = forward(0, 0, GROUP)
    t_share.ready()
    t_here.wait()

    aheads = []
    for n in range(GROUP):
        px[n] = xb[n] + 0.5 * (tb[n] - xb[n] - acc[0, block(n)])
        if n < REACH_DEV:
            aheads.append(move.to(px.at[n], ahead.at[n], before))
    set_x(REACH_DEV, px[REACH_DEV])
    final[REACH_DEV] = px[REACH_DEV]

    def settle(n):
        if n < REACH_DEV:
            rets[n].wait_recv()
            now = px[n] - 0.5 * ret_in[0, n]
            set_x(n, now)
            final[n] = now

    rets_last = outgoing(1, settle)
    settle(0)
    for a in range(GROUP):
        acc[1, block(a)] = forward(a, 0, GROUP - a)
    for a in range(REACH_DEV):
        inside(1, a)

    base = move.reserve(GROUP)
    here_sem = local_sem.at[move.local]

    def leave(n, source):
        return move.make(final.at[n], out.at[:, piece(j)], chip(n), base + n, base + source)

    def stay(n):
        return pltpu.make_async_copy(final.at[n], out.at[:, piece(j)], here_sem)

    def put(n):
        change = acc[1, block(n)]
        if n < REACH_DEV:
            rets_last[n].wait_recv()
            change = change + ret_in[1, n]
        final[n] = final[n] + 0.5 * (tb[n] - final[n] - change)

        @pl.when(j != n)
        def _():
            leave(n, j).start()

        @pl.when(j == n)
        def _():
            stay(n).start()

    for n in range(REACH_DEV):
        aheads[n].wait_recv()
        set_x(GROUP + n, ahead[n] - 0.5 * acc[0, block(GROUP + n)])
        for a in range(n + 1, GROUP):
            acc[1, block(a)] += forward(a, GROUP + n - a, 1)
    for n in (3, 2, 1, 0):
        put(n)
    for n in range(GROUP):
        @pl.when(j != n)
        def _():
            leave(n, n).wait_send()
            leave(n, n).wait_recv()

        @pl.when(j == n)
        def _():
            stay(n).wait()
    for copy in move.open:
        copy.wait_send()


def in_one_kernel(perturb, pair_list, pair_count, band_weight, cov_scale, target, first_guess):
    w = gap_weights(pair_list, pair_count, band_weight, cov_scale)
    table = jnp.broadcast_to(jnp.pad(w, (0, 8 - w.shape[0]))[:, None], (8, BLOCK))
    rows = perturb.shape[0]
    cols = first_guess.shape[1] // GROUP
    members = 2 * GROUP * PLANES * rows
    f32, bf16 = jnp.float32, jnp.bfloat16
    sems = 112
    vmem = pl.BlockSpec(memory_space=pltpu.VMEM)
    anywhere = pl.BlockSpec(memory_space=pl.ANY)
    return pl.pallas_call(
        kernel,
        out_shape=jax.ShapeDtypeStruct(first_guess.shape, f32),
        in_specs=[anywhere, vmem, anywhere, anywhere],
        out_specs=vmem,
        scratch_shapes=[
            pltpu.VMEM((PLANES, GROUP, 2, rows, 2 * REACH_DEV * BLOCK), f32),
            pltpu.VMEM((GROUP, 2, PLANES, rows, BLOCK), f32),
            pltpu.VMEM((members, 2 * REACH_DEV * BLOCK), bf16),
            pltpu.VMEM((members, 2 * REACH_DEV * BLOCK), bf16),
            pltpu.VMEM((members, BLOCK), bf16),
            pltpu.VMEM((members, BLOCK), bf16),
            pltpu.VMEM((REACH_DEV, BLOCK, GROUP * BLOCK), f32),
            pltpu.VMEM((GROUP, BLOCK, GROUP * BLOCK), bf16),
            pltpu.VMEM((GROUP, BLOCK, GROUP * BLOCK), bf16),
            pltpu.VMEM((GROUP, 8, BLOCK), f32),
            pltpu.VMEM((GROUP, BLOCK, cols), f32),
            pltpu.VMEM((GROUP, BLOCK, cols), f32),
            pltpu.VMEM((REACH_DEV, BLOCK, cols), f32),
            pltpu.VMEM((NEAR * BLOCK, 2 * cols), bf16),
            pltpu.VMEM((2, NEAR * BLOCK, cols), f32),
            pltpu.VMEM((GROUP, BLOCK, cols), f32),
            pltpu.VMEM((2, REACH_DEV, BLOCK, cols), f32),
            pltpu.VMEM((REACH_DEV, BLOCK, cols), f32),
            pltpu.VMEM((GROUP, BLOCK, cols), f32),
            pltpu.VMEM((2, 2, BLOCK // 2, cols), f32),
            pltpu.SemaphoreType.DMA((sems,)),
            pltpu.SemaphoreType.DMA((sems,)),
            pltpu.SemaphoreType.DMA((8,)),
        ],
        compiler_params=pltpu.CompilerParams(
            collective_id=0, has_side_effects=True, vmem_limit_bytes=56 * 1024 * 1024
        ),
    )(perturb, table, first_guess, target)


def fits(perturb, field):
    return (
        lax.axis_size("mem") == 2 and lax.axis_size("space") == PLANES * GROUP
        and perturb.shape[0] % 16 == 0 and field.shape[1] % (GROUP * 128) == 0
        and field.shape[0] == BLOCK
    )


def per_device(perturb, pair_list, pair_count, band_weight, cov_scale, target, first_guess):
    whole = in_one_kernel if fits(perturb, first_guess) else by_collectives
    return whole(perturb, pair_list, pair_count, band_weight, cov_scale, target, first_guess)


def solution(mesh):
    in_specs = (
        P(("space", "mem"), None),
        P("space", None),
        P("space"),
        P(),
        P(),
        P("space", "mem"),
        P("space", "mem"),
    )
    out_specs = P("space", "mem")
    return jax.shard_map(
        per_device, mesh=mesh, in_specs=in_specs, out_specs=out_specs, check_vma=False
    )
```

```python
import functools
import jax
import jax.numpy as jnp
from jax import lax
from jax.experimental import pallas as pl
from jax.experimental.pallas import tpu as pltpu
from jax.sharding import PartitionSpec as P

BLOCK = 256
MEMBERS = 1024
REACH_DEV = 3
NBANDS = 8
ITERS = 2


def shifted(array, axis, by):
    count = lax.axis_size(axis)
    return lax.ppermute(array, axis, [(i, (i + by) % count) for i in range(count)])


def mm(a, b, ca, cb):
    return lax.dot_general(
        a, b, (((ca,), (cb,)), ((), ())), precision=lax.Precision.HIGH,
        preferred_element_type=jnp.float32,
    )


def member_sum(tile):
    if lax.axis_size("mem") == 2:
        return tile + shifted(tile, "mem", 1)
    return lax.psum(tile, "mem")


def gap_weights(pair_list, pair_count, band_weight, cov_scale):
    slots = pair_list.shape[0]
    blocks_all = lax.axis_size("space")
    gap = (pair_list[:, 1] - pair_list[:, 0]) % blocks_all
    living = (jnp.arange(slots, dtype=jnp.int32) < pair_count[0]).astype(jnp.float32)
    bands = jnp.arange(NBANDS, dtype=jnp.int32)
    band_now = jnp.sum(
        jnp.where(pair_list[:, 2][:, None] == bands[None, :], band_weight[None, :], 0.0), axis=1
    )
    slot_weight = cov_scale[0] * band_now * living / (MEMBERS - 1)
    gaps = jnp.arange(REACH_DEV + 1, dtype=jnp.int32)
    return jnp.sum(jnp.where(gap[:, None] == gaps[None, :], slot_weight[:, None], 0.0), axis=0)


def by_collectives(perturb, pair_list, pair_count, band_weight, cov_scale, target, first_guess):
    w = gap_weights(pair_list, pair_count, band_weight, cov_scale)
    w_next = shifted(w, "space", -1)
    p0 = lax.all_to_all(perturb, "space", split_axis=1, concat_axis=0, tiled=True)
    p1 = shifted(p0, "space", -1)
    p3 = shifted(p0, "space", -3)
    x0 = first_guess
    t0 = mm(p0, p0, 0, 0) * w[0]
    t1 = mm(p0, p1, 0, 0) * w[1]
    t3 = mm(p0, p3, 0, 0) * w[3]
    t2 = mm(p1, p3, 0, 0) * w_next[2]
    t0, t1, t2, t3 = (member_sum(t) for t in (t0, t1, t2, t3))
    for sweep in range(ITERS):
        x1 = shifted(x0, "space", -1)
        x3 = shifted(x0, "space", -3)
        back1 = shifted(mm(t1, x0, 0, 0) + mm(t2, x3, 1, 0), "space", 1)
        back3 = shifted(mm(t3, x0, 0, 0) + mm(t2, x1, 0, 0), "space", 3)
        own = mm(t0, x0, 1, 0) + mm(t1, x1, 1, 0) + mm(t3, x3, 1, 0)
        x0 = x0 + 0.5 * (target - x0 - (own + back1 + back3))
    return x0

GROUP = REACH_DEV + 1
NEAR = 2 * REACH_DEV + 1
PLANES = 4


def split(value):
    high = value.astype(jnp.bfloat16)
    return high, (value - high.astype(jnp.float32)).astype(jnp.bfloat16)


def dot(a, b, ca, cb):
    return lax.dot_general(a, b, (((ca,), (cb,)), ((), ())), preferred_element_type=jnp.float32)


class Mover:
    def __init__(self, send_sem, recv_sem, local_sem):
        self.send_sem, self.recv_sem, self.local_sem = send_sem, recv_sem, local_sem
        self.used = 0
        self.local = 0
        self.open = []

    def reserve(self, number):
        first = self.used
        self.used += number
        return first

    def make(self, source, target, device, send, recv):
        return pltpu.make_async_remote_copy(
            src_ref=source, dst_ref=target,
            send_sem=self.send_sem.at[send], recv_sem=self.recv_sem.at[recv],
            device_id=device, device_id_type=pl.DeviceIdType.MESH,
        )

    def to(self, source, target, device, send=None, recv=None):
        if send is None:
            send = recv = self.reserve(1)
        copy = self.make(source, target, device, send, recv)
        copy.start()
        self.open.append(copy)
        return copy

    def here(self, source, target):
        copy = pltpu.make_async_copy(source, target, self.local_sem.at[self.local])
        self.local += 1
        copy.start()
        return copy


def kernel(perturb, pair_list, pair_count, band_weight, cov_scale, guess, target, out, gc, gb, chi, clo, bhi, blo, part, tile_hi, tile_lo,
           tabs, xb, tb, halo, xs, acc, px, ret_in, ahead, final, via, pairs, live, bands,
           scale, send_sem, recv_sem, local_sem):
    space = lax.axis_index("space")
    mem = lax.axis_index("mem")
    k = space // GROUP
    j = space % GROUP
    rows = perturb.shape[0]
    half = rows // 2
    cols = xb.shape[2]
    B = BLOCK
    wide = REACH_DEV * B
    inner = GROUP * B
    each = 2 * GROUP * rows

    def plane(p):
        return (p * GROUP + j, mem)

    def chip(q):
        return (k * GROUP + q, mem)

    xn = chip(j + 1 - 2 * (j % 2))
    yn = chip((j + 2) % GROUP)
    partner = (space, 1 - mem)
    before = plane((k + PLANES - 1) % PLANES)
    after = plane((k + 1) % PLANES)

    barrier = pltpu.get_barrier_semaphore()
    greeted = [plane((k + r) % PLANES) for r in range(1, PLANES)]
    greeted += [chip((j + q) % GROUP) for q in range(1, GROUP)] + [partner]
    for device in greeted:
        pl.semaphore_signal(barrier, inc=1, device_id=device, device_id_type=pl.DeviceIdType.MESH)

    move = Mover(send_sem, recv_sem, local_sem)

    def at(block, size):
        return pl.ds(pl.multiple_of(block * B, B), size * B)

    def piece(q):
        return pl.ds(pl.multiple_of(q * cols, cols), cols)

    def pieces(p, slot):
        first = p * GROUP
        after_first = ((p + 1) % PLANES) * GROUP
        return (
            (perturb.at[:, at(first + 1, REACH_DEV)], gc.at[slot, 0, 0, :, pl.ds(0, wide)]),
            (perturb.at[:, at(after_first, REACH_DEV)], gc.at[slot, 0, 0, :, pl.ds(wide, wide)]),
            (perturb.at[:, at(first, 1)], gb.at[0, 0, slot]),
        )

    own_here = [move.here(*pair) for pair in pieces(k, 0)]
    x_here = move.here(guess.at[:, piece(j)], xb.at[j])
    t_here = move.here(target.at[:, piece(j)], tb.at[j])
    small = [move.here(pair_list, pairs), move.here(pair_count, live),
             move.here(band_weight, bands), move.here(cov_scale, scale)]
    pl.semaphore_wait(barrier, len(greeted))

    zsem = move.reserve(3 * PLANES)
    other_half = 2 - 2 * (k // 2)
    late = 2 + (k + k // 2 + 1) % 2
    routes = ((k + 1 - 2 * (k % 2), 1), (other_half, late), (other_half + 1, late))

    def exchange(which):
        for n, (p, slot) in enumerate(routes):
            for m in which:
                source, place = pieces(p, slot)[m]
                move.to(source, place, plane(p), zsem + 3 * n + m, zsem + 3 * slot + m)

    def from_plane(slot, which):
        for m in which:
            place = pieces(k, slot)[m][1]
            move.make(place, place, before, zsem, zsem + 3 * slot + m).wait_recv()

    exchange((0, 1))
    for copy in own_here:
        copy.wait()

    class Gather:
        def __init__(self, buffer, cut):
            self.buffer, self.cut = buffer, cut

        def own(self):
            source = self.buffer.at[0, 0]
            self.cx = move.to(source, self.buffer.at[1, 0], xn)
            self.cy = move.to(source, self.buffer.at[2, 0], yn)
            self.done = [move.to(source, self.buffer.at[0, 1], partner)]

        def over(self, q):
            self.done.append(move.to(self.buffer.at[q, 0], self.buffer.at[q, 1], partner))

        def relay(self):
            low, high = pl.ds(0, self.cut), pl.ds(self.cut, self.cut)
            self.cx.wait_recv()
            first = move.to(self.buffer.at[1, 0, low], self.buffer.at[3, 0, low], yn)
            self.over(1)
            self.cy.wait_recv()
            second = move.to(self.buffer.at[2, 0, high], self.buffer.at[3, 0, high], xn)
            self.over(2)
            self.halves = (first, second)

        def corner(self):
            for copy in self.halves:
                copy.wait_recv()
            self.over(3)

        def ready(self):
            for copy in self.done:
                copy.wait_recv()

    cross = [Gather(gc.at[r], half) for r in range(PLANES)]
    edge = Gather(gb, PLANES // 2)
    cross[0].own()
    for copy in small:
        copy.wait()
    sums = [0.0] * GROUP
    for n in range(pairs.shape[0]):
        gap = (pairs[n, 1] - pairs[n, 0] + PLANES * GROUP) % (PLANES * GROUP)
        band = pairs[n, 2]
        rate = jnp.float32(0.0)
        for c in range(NBANDS):
            rate = jnp.where(band == c, bands[c], rate)
        rate = jnp.where(n < live[0], rate * scale[0], 0.0)
        sums = [jnp.where(gap == d, rate, sums[d]) for d in range(GROUP)]
    line = lax.broadcasted_iota(jnp.int32, (8, B), 0)
    rates = jnp.zeros((8, B), jnp.float32)
    for d in range(GROUP):
        rates = jnp.where(line == d, sums[d], rates)
    tabs[j] = rates / (MEMBERS - 1)
    tab_copies = [move.to(tabs.at[j], tabs.at[j], chip((j + q) % GROUP)) for q in range(1, GROUP)]

    jx = j + 1 - 2 * (j % 2)
    jy = (j + 2) % GROUP
    jd = (jx + 2) % GROUP
    top, bottom = pl.ds(0, B // 2), pl.ds(B // 2, B // 2)

    class Share:
        def __init__(self, source, blocks, via):
            self.blocks, self.via = blocks, via
            self.first = move.to(source.at[top, piece(jd)], via.at[0], xn)
            self.second = move.to(source.at[bottom, piece(jd)], via.at[1], yn)
            self.done = [move.to(source.at[:, piece(jx)], blocks.at[j], xn),
                         move.to(source.at[:, piece(jy)], blocks.at[j], yn)]

        def relay(self):
            self.first.wait_recv()
            self.done.append(move.to(self.via.at[0], self.blocks.at[jx, top], yn))
            self.second.wait_recv()
            self.done.append(move.to(self.via.at[1], self.blocks.at[jy, bottom], xn))

        def ready(self):
            for copy in self.done:
                copy.wait_recv()

    x_share = Share(guess, xb, via.at[0])
    exchange((2,))

    def weight(a, d):
        return tabs[a, d : d + 1]

    def pair(span, n, first, size):
        own = pl.ds(pl.multiple_of(n * B, B), B)
        row = pl.ds(pl.multiple_of((n + first) * B, B), size * B)
        left = jnp.concatenate([chi[span, own], chi[span, own], clo[span, own]], 0)
        right = jnp.concatenate([chi[span, row], clo[span, row], chi[span, row]], 0)
        return dot(left, right, 0, 0)

    def members(r):
        span = pl.ds(r * each, each)
        chi[span], clo[span] = split(gc[r].reshape(each, 2 * wide))
        return span

    def products(r):
        span = members(r)

        def step(n, carry):
            value = pair(span, n, 0, GROUP)
            part[n] = value if r == 0 else part[n] + value
            return carry

        lax.fori_loop(0, REACH_DEV, step, 0)

    def finish(span, a, first, size):
        value = pair(span, a - 1, first, size) + part[a - 1, :, pl.ds(first * B, size * B)]
        for d in range(size):
            now = value[:, d * B : (d + 1) * B] * weight(a, first + d)
            there = pl.ds((first + d) * B, B)
            tile_hi[a, :, there], tile_lo[a, :, there] = split(now)

    def edge_products():
        for r in range(PLANES):
            span = pl.ds(r * each, each)
            bhi[span], blo[span] = split(gb[:, :, r].reshape(each, B))
        left = jnp.concatenate([bhi[...], bhi[...], blo[...]], 0)
        right = jnp.concatenate([bhi[...], blo[...], bhi[...]], 0)
        now = dot(left, right, 0, 0) * weight(0, 0)
        tile_hi[0, :, :B], tile_lo[0, :, :B] = split(now)
        for d in range(1, GROUP):
            there = pl.ds((d - 1) * B, B)
            right = jnp.concatenate([chi[:, there], clo[:, there], chi[:, there]], 0)
            now = dot(left, right, 0, 0) * weight(0, d)
            place = pl.ds(d * B, B)
            tile_hi[0, :, place], tile_lo[0, :, place] = split(now)

    def times(high, low, x, side):
        both = dot(high, x, side, 0)
        return both[:, :cols] + both[:, cols:] + dot(low, x[:, :cols], side, 0)

    def block(n, size=1):
        return pl.ds(n * B, size * B)

    def set_x(n, value):
        xs[block(n), :cols], xs[block(n), cols:] = split(value)

    def forward(a, d, size):
        span = pl.ds(d * B, size * B)
        return times(tile_hi[a, :, span], tile_lo[a, :, span], xs[block(a + d, size)], 1)

    def down(a, first, size):
        span = pl.ds(first * B, size * B)
        return times(tile_hi[a, :, span], tile_lo[a, :, span], xs[block(a)], 0)

    def outgoing(sweep, ready):
        copies = {}
        for n in range(REACH_DEV - 1, -1, -1):
            a = n + 1
            ready(a)
            value = down(a, GROUP - a, a)
            if a == REACH_DEV:
                acc[sweep, block(GROUP, a)] = value
            else:
                acc[sweep, block(GROUP, a)] += value
            copies[n] = move.to(acc.at[sweep, block(GROUP + n)], ret_in.at[sweep, n], after)
        return copies

    def inside(sweep, a):
        acc[sweep, block(a + 1, REACH_DEV - a)] += down(a, 1, REACH_DEV - a)

    for slot in range(1, PLANES):
        from_plane(slot, (0, 1))
        cross[slot].own()
        cross[slot - 1].relay()
        if slot == 1:
            x_share.relay()
        if slot >= 2:
            cross[slot - 2].corner()
        if slot == 2:
            x_share.ready()
            x_here.wait()
            halo_copy = move.to(xb.at[pl.ds(0, REACH_DEV)], halo, before)
    for slot in range(1, PLANES):
        from_plane(slot, (2,))
    edge.own()
    for n in range(GROUP):
        set_x(n, xb[n])
    cross[0].ready()
    products(0)
    cross[1].ready()
    products(1)
    cross[3].relay()
    cross[2].corner()
    cross[2].ready()
    products(2)
    edge.relay()
    t_share = Share(target, tb, via.at[1])
    for copy in tab_copies:
        copy.wait_recv()
    cross[3].corner()
    cross[3].ready()
    last = members(PLANES - 1)
    for a in range(REACH_DEV, 0, -1):
        finish(last, a, GROUP - a, a)
    rets = outgoing(0, lambda a: None)
    t_share.relay()
    halo_copy.wait_recv()
    for n in range(REACH_DEV):
        set_x(GROUP + n, halo[n])
    for a in range(1, GROUP):
        finish(last, a, 0, GROUP - a)
    for a in range(1, GROUP):
        acc[0, block(a)] = forward(a, 0, GROUP)
    inside(0, 1)
    inside(0, 2)
    edge.corner()
    edge.ready()
    edge_products()
    inside(0, 0)
    acc[0, block(0)] = forward(0, 0, GROUP)
    t_share.ready()
    t_here.wait()

    aheads = []
    for n in range(GROUP):
        px[n] = xb[n] + 0.5 * (tb[n] - xb[n] - acc[0, block(n)])
        if n < REACH_DEV:
            aheads.append(move.to(px.at[n], ahead.at[n], before))
    set_x(REACH_DEV, px[REACH_DEV])
    final[REACH_DEV] = px[REACH_DEV]

    def settle(n):
        if n < REACH_DEV:
            rets[n].wait_recv()
            now = px[n] - 0.5 * ret_in[0, n]
            set_x(n, now)
            final[n] = now

    rets_last = outgoing(1, settle)
    settle(0)
    for a in range(GROUP):
        acc[1, block(a)] = forward(a, 0, GROUP - a)
    for a in range(REACH_DEV):
        inside(1, a)

    base = move.reserve(GROUP)
    here_sem = local_sem.at[move.local]

    def leave(n, source):
        return move.make(final.at[n], out.at[:, piece(j)], chip(n), base + n, base + source)

    def stay(n):
        return pltpu.make_async_copy(final.at[n], out.at[:, piece(j)], here_sem)

    def put(n):
        change = acc[1, block(n)]
        if n < REACH_DEV:
            rets_last[n].wait_recv()
            change = change + ret_in[1, n]
        final[n] = final[n] + 0.5 * (tb[n] - final[n] - change)

        @pl.when(j != n)
        def _():
            leave(n, j).start()

        @pl.when(j == n)
        def _():
            stay(n).start()

    for n in range(REACH_DEV):
        aheads[n].wait_recv()
        set_x(GROUP + n, ahead[n] - 0.5 * acc[0, block(GROUP + n)])
        for a in range(n + 1, GROUP):
            acc[1, block(a)] += forward(a, GROUP + n - a, 1)
    for n in (3, 2, 1, 0):
        put(n)
    for n in range(GROUP):
        @pl.when(j != n)
        def _():
            leave(n, n).wait_send()
            leave(n, n).wait_recv()

        @pl.when(j == n)
        def _():
            stay(n).wait()
    for copy in move.open:
        copy.wait_send()


def in_one_kernel(perturb, pair_list, pair_count, band_weight, cov_scale, target, first_guess):
    rows = perturb.shape[0]
    cols = first_guess.shape[1] // GROUP
    members = 2 * GROUP * PLANES * rows
    f32, bf16 = jnp.float32, jnp.bfloat16
    sems = 112
    vmem = pl.BlockSpec(memory_space=pltpu.VMEM)
    anywhere = pl.BlockSpec(memory_space=pl.ANY)
    return pl.pallas_call(
        kernel,
        out_shape=jax.ShapeDtypeStruct(first_guess.shape, f32),
        in_specs=[anywhere] * 7,
        out_specs=vmem,
        scratch_shapes=[
            pltpu.VMEM((PLANES, GROUP, 2, rows, 2 * REACH_DEV * BLOCK), f32),
            pltpu.VMEM((GROUP, 2, PLANES, rows, BLOCK), f32),
            pltpu.VMEM((members, 2 * REACH_DEV * BLOCK), bf16),
            pltpu.VMEM((members, 2 * REACH_DEV * BLOCK), bf16),
            pltpu.VMEM((members, BLOCK), bf16),
            pltpu.VMEM((members, BLOCK), bf16),
            pltpu.VMEM((REACH_DEV, BLOCK, GROUP * BLOCK), f32),
            pltpu.VMEM((GROUP, BLOCK, GROUP * BLOCK), bf16),
            pltpu.VMEM((GROUP, BLOCK, GROUP * BLOCK), bf16),
            pltpu.VMEM((GROUP, 8, BLOCK), f32),
            pltpu.VMEM((GROUP, BLOCK, cols), f32),
            pltpu.VMEM((GROUP, BLOCK, cols), f32),
            pltpu.VMEM((REACH_DEV, BLOCK, cols), f32),
            pltpu.VMEM((NEAR * BLOCK, 2 * cols), bf16),
            pltpu.VMEM((2, NEAR * BLOCK, cols), f32),
            pltpu.VMEM((GROUP, BLOCK, cols), f32),
            pltpu.VMEM((2, REACH_DEV, BLOCK, cols), f32),
            pltpu.VMEM((REACH_DEV, BLOCK, cols), f32),
            pltpu.VMEM((GROUP, BLOCK, cols), f32),
            pltpu.VMEM((2, 2, BLOCK // 2, cols), f32),
            pltpu.SMEM(pair_list.shape, jnp.int32),
            pltpu.SMEM(pair_count.shape, jnp.int32),
            pltpu.SMEM(band_weight.shape, f32),
            pltpu.SMEM(cov_scale.shape, f32),
            pltpu.SemaphoreType.DMA((sems,)),
            pltpu.SemaphoreType.DMA((sems,)),
            pltpu.SemaphoreType.DMA((16,)),
        ],
        compiler_params=pltpu.CompilerParams(
            collective_id=0, has_side_effects=True, vmem_limit_bytes=56 * 1024 * 1024
        ),
    )(perturb, pair_list, pair_count, band_weight, cov_scale, first_guess, target)


def fits(perturb, field):
    return (
        lax.axis_size("mem") == 2 and lax.axis_size("space") == PLANES * GROUP
        and perturb.shape[0] % 16 == 0 and field.shape[1] % (GROUP * 128) == 0
        and field.shape[0] == BLOCK
    )


def per_device(perturb, pair_list, pair_count, band_weight, cov_scale, target, first_guess):
    whole = in_one_kernel if fits(perturb, first_guess) else by_collectives
    return whole(perturb, pair_list, pair_count, band_weight, cov_scale, target, first_guess)


def solution(mesh):
    in_specs = (
        P(("space", "mem"), None),
        P("space", None),
        P("space"),
        P(),
        P(),
        P("space", "mem"),
        P("space", "mem"),
    )
    out_specs = P("space", "mem")
    return jax.shard_map(
        per_device, mesh=mesh, in_specs=in_specs, out_specs=out_specs, check_vma=False
    )
```
